256 devices in a mesh: shot: 8 (over x, y_lo), domain: 32 (over z, y_hi, core).
Axes of the slice: x: 4, y: 4 (y_hi: 2, y_lo: 2; y = y_hi * 2 + y_lo), z: 8, core: 2. Of those that a mesh axis runs over, the one named last changes fastest.
Arguments:
- velsq: float32 [64, 256, 128], P('domain', 'shot'), may hold values from 0.04 to 0.12
- epsilon: float32 [64, 256, 128], P('domain', 'shot'), may hold values from 0 to 0.3
- delta: float32 [64, 256, 128], P('domain', 'shot'), may hold values from 0 to 0.15
- tilt: float32 [64, 256, 128], P('domain', 'shot'), may hold values from -1.2 to 1.2
- azimuth: float32 [64, 256, 128], P('domain', 'shot'), may hold values from -3.140625 to 3.140625
- forward_state: float32 [8, 4, 64, 256, 128], P('shot', None, 'domain'), may hold values from -6 to 6
- adjoint_state: float32 [8, 4, 64, 256, 128], P('shot', None, 'domain'), may hold values from -6 to 6
- wavelet: float32 [8, 2], P('shot'), may hold values from -60 to 60
- source: int32 [8], P('shot'), may hold values from 0 to 2097151
- receivers: int32 [8, 256], P('shot'), may hold values from 0 to 2097151
- observed: float32 [8, 2, 256], P('shot'), may hold values from -18 to 18
Outputs:
- gradients: float32 [5, 64, 256, 128], P(None, 'domain', 'shot')
The draws below stay inside these ranges and needn't reach their ends.
Inputs may be any that keep to these rules, and one draw needn't show every extreme that they name: `source`: flat index x * 256 * 128 + y * 128 + z of a grid cell. `receivers`: flat index x * 256 * 128 + y * 128 + z of a grid cell; cells may repeat.
All inputs are finite; a program needn't handle non-finite values.
Results may differ from the reference program's by a relative error of at most 0.0001.
Values sent between devices are 32-bit elements; how exact they have to be, the bound alone decides.
A program may use at most 128 MiB of HBM per device.

```python
import math
import jax
import jax.numpy as jnp
from jax import lax

NY = 256
NZ = 128
STEPS = 2
REC = 256
NX = 64
SHOTS = 8


def set_ends(drawn, key, low, high):
    extent = drawn.shape
    index_at = [jax.random.randint(jax.random.fold_in(key, axis), (), 0, extent[axis]) for axis in range(len(extent))]
    drawn = drawn.at[tuple(index_at)].set(low)
    longest = extent.index(max(extent))
    index_at[longest] = (index_at[longest] + 1) % extent[longest]
    return drawn.at[tuple(index_at)].set(high)


def steps_of(key, shape, cuts, smallest, largest):
    factor_of = 1.0
    for axis_at, parts in cuts:
        draws = jax.random.uniform(jax.random.fold_in(jax.random.fold_in(key, 6), axis_at), (parts,), jnp.float32, smallest / len(cuts), largest / len(cuts))
        factor_of = factor_of * jnp.repeat(jnp.exp(draws), shape[axis_at] // parts).reshape((-1,) + (1,) * (len(shape) - 1 - axis_at))
    return factor_of


def noise(rng, shape, width, limit, split=(), dtype=jnp.bfloat16):
    gain = steps_of(rng, shape, split, -0.22, 0.18) if split else 1.0
    drawn = jax.random.normal(rng, shape, jnp.float32) * width * gain
    return jnp.minimum(jnp.maximum(drawn, -limit), limit).astype(dtype)


def setup_inputs(seed: int = 0) -> dict:
    key_of = jax.random.split(jax.random.key(seed), 12)
    velsq = jnp.clip(jnp.exp(math.log(0.12) - 1.0986123 * jax.random.uniform(key_of[0], (NX, NY, NZ), jnp.float32) ** steps_of(key_of[0], (NX, NY, NZ), ((0, 32), (1, 8)), -0.2, 0.2)), 0.04, 0.12)
    epsilon = jnp.clip(0.3 * jax.random.uniform(key_of[1], (NX, NY, NZ), jnp.float32) ** steps_of(key_of[1], (NX, NY, NZ), ((0, 32), (1, 8)), -0.2, 0.2), 0.0, 0.3)
    delta = jnp.clip(0.15 * jax.random.uniform(key_of[2], (NX, NY, NZ), jnp.float32) ** steps_of(key_of[2], (NX, NY, NZ), ((0, 32), (1, 8)), -0.2, 0.2), 0.0, 0.15)
    tilt = jnp.clip(jax.random.uniform(key_of[3], (NX, NY, NZ), jnp.float32, -1.2, 1.2) * steps_of(key_of[3], (NX, NY, NZ), ((0, 32), (1, 8)), -0.4, 0.0), -1.2, 1.2)
    azimuth = jnp.clip(jax.random.uniform(key_of[4], (NX, NY, NZ), jnp.float32, -3.140625, 3.140625), -3.140625, 3.140625)
    forward_state = noise(key_of[5], (SHOTS, 4, NX, NY, NZ), 1.0, 6.0, ((0, 8), (2, 32)), jnp.float32)
    adjoint_state = noise(key_of[6], (SHOTS, 4, NX, NY, NZ), 1.0, 6.0, ((0, 8), (2, 32)), jnp.float32)
    wavelet = noise(key_of[7], (SHOTS, STEPS), 10.0, 60.0, ((0, 8),), jnp.float32)
    source = set_ends(jax.random.randint(key_of[8], (SHOTS,), 0, NX * NY * NZ), jax.random.fold_in(key_of[8], 1), 0, (NX * NY * NZ) - 1).astype(jnp.int32)
    receivers = set_ends(jax.random.randint(key_of[9], (SHOTS, REC), 0, NX * NY * NZ), jax.random.fold_in(key_of[9], 1), 0, (NX * NY * NZ) - 1).astype(jnp.int32)
    observed = noise(key_of[10], (SHOTS, STEPS, REC), 3.0, 18.0, ((0, 8),), jnp.float32)
    return {"velsq": velsq, "epsilon": epsilon, "delta": delta, "tilt": tilt, "azimuth": azimuth, "forward_state": forward_state, "adjoint_state": adjoint_state, "wavelet": wavelet, "source": source, "receivers": receivers, "observed": observed}


def hessian(values):
    padded = jnp.pad(values, ((0, 0), (1, 1), (1, 1)))
    center = padded[1:-1, 1:-1, 1:-1]
    curve_xx = padded[2:, 1:-1, 1:-1] + padded[:-2, 1:-1, 1:-1] - 2.0 * center
    curve_yy = padded[1:-1, 2:, 1:-1] + padded[1:-1, :-2, 1:-1] - 2.0 * center
    curve_zz = padded[1:-1, 1:-1, 2:] + padded[1:-1, 1:-1, :-2] - 2.0 * center
    mixed_xy = 0.25 * (padded[2:, 2:, 1:-1] - padded[2:, :-2, 1:-1] - padded[:-2, 2:, 1:-1] + padded[:-2, :-2, 1:-1])
    mixed_xz = 0.25 * (padded[2:, 1:-1, 2:] - padded[2:, 1:-1, :-2] - padded[:-2, 1:-1, 2:] + padded[:-2, 1:-1, :-2])
    mixed_yz = 0.25 * (padded[1:-1, 2:, 2:] - padded[1:-1, 2:, :-2] - padded[1:-1, :-2, 2:] + padded[1:-1, :-2, :-2])
    return jnp.stack([curve_xx, curve_yy, curve_zz, mixed_xy, mixed_xz, mixed_yz])

def tables(velsq, epsilon, delta, tilt, azimuth):
    sin_tilt = jnp.sin(tilt)
    cos_tilt = jnp.cos(tilt)
    sin_azim = jnp.sin(azimuth)
    cos_azim = jnp.cos(azimuth)
    axis_x = sin_tilt * cos_azim
    axis_y = sin_tilt * sin_azim
    axis_z = cos_tilt
    turn_x = cos_tilt * cos_azim
    turn_y = cos_tilt * sin_azim
    turn_z = -sin_tilt
    spin_x = -sin_tilt * sin_azim
    spin_y = sin_tilt * cos_azim
    along = jnp.stack([axis_x * axis_x, axis_y * axis_y, axis_z * axis_z, 2.0 * axis_x * axis_y, 2.0 * axis_x * axis_z, 2.0 * axis_y * axis_z])
    by_tilt = jnp.stack([2.0 * turn_x * axis_x, 2.0 * turn_y * axis_y, 2.0 * turn_z * axis_z, 2.0 * (turn_x * axis_y + turn_y * axis_x), 2.0 * (turn_x * axis_z + turn_z * axis_x), 2.0 * (turn_y * axis_z + turn_z * axis_y)])
    by_spin = jnp.stack([2.0 * spin_x * axis_x, 2.0 * spin_y * axis_y, jnp.zeros_like(axis_z), 2.0 * (spin_x * axis_y + spin_y * axis_x), 2.0 * spin_x * axis_z, 2.0 * spin_y * axis_z])
    return (velsq, 1.0 + 2.0 * epsilon, jnp.sqrt(1.0 + 2.0 * delta), along, by_tilt, by_spin)

def operate(pad_p, pad_q, table, full):
    speed_sq, stretch, root_d, along, by_tilt, by_spin = table
    hess_p = hessian(pad_p)
    hess_q = hessian(pad_q)
    laplace = hess_p[0] + hess_p[1] + hess_p[2]
    axial_p = lax.optimization_barrier(jnp.sum(along * hess_p, axis=0))
    axial_q = lax.optimization_barrier(jnp.sum(along * hess_q, axis=0))
    across = laplace - axial_p
    drive_p = stretch * across + root_d * axial_q
    drive_q = root_d * across + axial_q
    if full:
        image_terms = (across, axial_q, lax.optimization_barrier(jnp.sum(by_tilt * hess_p, axis=0)), lax.optimization_barrier(jnp.sum(by_tilt * hess_q, axis=0)), lax.optimization_barrier(jnp.sum(by_spin * hess_p, axis=0)), lax.optimization_barrier(jnp.sum(by_spin * hess_q, axis=0)))
        return (drive_p, drive_q, image_terms)
    return (drive_p, drive_q, ())

def advance(pad_p, pad_q, prior_p, prior_q, table, full):
    drive_p, drive_q, image_terms = operate(pad_p, pad_q, table, full)
    speed_sq = table[0]
    next_p = 2.0 * pad_p[1:-1] - prior_p + speed_sq * drive_p
    next_q = 2.0 * pad_q[1:-1] - prior_q + speed_sq * drive_q
    return (next_p, next_q, image_terms)

def correlate(gradient, adjoint_p, adjoint_q, image_terms, table):
    speed_sq, stretch, root_d, along, by_tilt, by_spin = table
    across, axial_q, tilt_p, tilt_q, spin_p, spin_q = image_terms
    g_speed = gradient[0] + adjoint_p * (stretch * across + root_d * axial_q) + adjoint_q * (root_d * across + axial_q)
    g_eps = gradient[1] + 2.0 * speed_sq * adjoint_p * across
    g_delta = gradient[2] + speed_sq * (adjoint_p * axial_q + adjoint_q * across) / root_d
    g_tilt = gradient[3] + speed_sq * (adjoint_p * (root_d * tilt_q - stretch * tilt_p) + adjoint_q * (tilt_q - root_d * tilt_p))
    g_spin = gradient[4] + speed_sq * (adjoint_p * (root_d * spin_q - stretch * spin_p) + adjoint_q * (spin_q - root_d * spin_p))
    return (g_speed, g_eps, g_delta, g_tilt, g_spin)

def pad_rows(values):
    return jnp.pad(values, ((1, 1), (0, 0), (0, 0)))

def shot_gradient(table, start_state, end_state, wave_row, source_cell, receiver_cells, observed_trace):
    older_p, field_p, older_q, field_q = (start_state[0], start_state[1], start_state[2], start_state[3])
    layout = field_p.shape
    saved = []
    traces = []
    for moment in range(STEPS):
        next_p, next_q, image_terms = advance(pad_rows(field_p), pad_rows(field_q), older_p, older_q, table, True)
        next_p = next_p.reshape(-1).at[source_cell].add(wave_row[moment]).reshape(layout)
        next_q = next_q.reshape(-1).at[source_cell].add(wave_row[moment]).reshape(layout)
        saved.append(image_terms)
        traces.append(next_p.reshape(-1)[receiver_cells])
        older_p, field_p, older_q, field_q = (field_p, next_p, field_q, next_q)
    misfit = jnp.stack(traces) - observed_trace
    before_p, adjoint_p, before_q, adjoint_q = (end_state[0], end_state[1], end_state[2], end_state[3])
    gradient = tuple((jnp.zeros(layout, jnp.float32) for member in range(5)))
    for moment in range(STEPS):
        back_index = STEPS - 1 - moment
        gradient = correlate(gradient, adjoint_p, adjoint_q, saved[back_index], table)
        next_p, next_q, unused = advance(pad_rows(adjoint_p), pad_rows(adjoint_q), before_p, before_q, table, False)
        next_p = next_p.reshape(-1).at[receiver_cells].add(misfit[back_index]).reshape(layout)
        before_p, adjoint_p, before_q, adjoint_q = (adjoint_p, next_p, adjoint_q, next_q)
    return jnp.stack(gradient)

def reference(velsq, epsilon, delta, tilt, azimuth, forward_state, adjoint_state, wavelet, source, receivers, observed):
    table = tables(velsq, epsilon, delta, tilt, azimuth)
    summed = jnp.zeros((5,) + velsq.shape, jnp.float32)

    def per_shot(carry, shot_inputs):
        start_state, end_state, wave_row, source_cell, receiver_cells, observed_trace = shot_inputs
        return (carry + shot_gradient(table, start_state, end_state, wave_row, source_cell, receiver_cells, observed_trace), None)
    summed, unused = lax.scan(per_shot, summed, (forward_state, adjoint_state, wavelet, source, receivers, observed))
    return summed
```

```python
import functools

import jax
import jax.numpy as jnp
from jax import lax
from jax.experimental import pallas as pl
from jax.experimental.pallas import tpu as pltpu
from jax.sharding import PartitionSpec as P

MESH = pl.DeviceIdType.MESH
TILE = 8
PAD = 8

PEERS = ((0, 1), (1, 0), (3, 0), (1, 1), (3, 1), (2, 0), (2, 1))
MIRROR = tuple(PEERS.index(((4 - dx) % 4, dy)) for dx, dy in PEERS)

SIN = (1.0, -1 / 6, 1 / 120, -1 / 5040, 1 / 362880, -1 / 39916800, 1 / 6227020800)
COS = (1.0, -1 / 2, 1 / 24, -1 / 720, 1 / 40320, -1 / 3628800, 1 / 479001600, -1 / 87178291200)


def horner(square, series):
    total = jnp.float32(series[-1])
    for term in series[-2::-1]:
        total = total * square + jnp.float32(term)
    return total


def sin_cos(angle):
    square = angle * angle
    return angle * horner(square, SIN), horner(square, COS)


def sin_cos_wide(angle):
    half_sin, half_cos = sin_cos(0.5 * angle)
    return 2.0 * half_sin * half_cos, 1.0 - 2.0 * half_sin * half_sin


def hessian(pad_ref, row, first, last):
    here = pad_ref[:, pl.ds(row, TILE), :]
    above = pad_ref[:, pl.ds(row + 1, TILE), :]
    below = pad_ref[:, pl.ds(row - 1, TILE), :]

    def ahead(values):
        return jnp.where(last, 0.0, pltpu.roll(values, values.shape[-1] - 1, 2))

    def behind(values):
        return jnp.where(first, 0.0, pltpu.roll(values, 1, 2))

    center = here[1:3]
    twice = 2.0 * center
    along_x = here[2:4] - here[0:2]
    along_y = above[1:3] - below[1:3]
    xx = here[2:4] + here[0:2] - twice
    yy = above[1:3] + below[1:3] - twice
    zz = ahead(center) + behind(center) - twice
    xy = (above[2:4] - above[0:2]) - (below[2:4] - below[0:2])
    xz = ahead(along_x) - behind(along_x)
    yz = ahead(along_y) - behind(along_y)
    return center, (xx, yy, zz, xy, xz, yz)


def times_axis(parts, axis, quarter):
    xx, yy, zz, xy, xz, yz = parts
    return (
        xx * axis[0] + xy * quarter[1] + xz * quarter[2],
        xy * quarter[0] + yy * axis[1] + yz * quarter[2],
        xz * quarter[0] + yz * quarter[1] + zz * axis[2],
    )


def dot3(left, right):
    return left[0] * right[0] + left[1] * right[1] + left[2] * right[2]


def kernel(
    velsq,
    epsilon,
    delta,
    tilt,
    azimuth,
    forward,
    adjoint,
    wavelet,
    source,
    receivers,
    observed,
    out,
    coef,
    pad_p,
    pad_q,
    pad_a,
    pad_b,
    pad_p1,
    pad_q1,
    olds,
    table,
    terms,
    step_a,
    hits,
    grad,
    parts,
    local_sem,
    gather_send,
    gather_recv,
    halo_send,
    halo_recv,
    next_send,
    next_recv,
    sum_send,
    sum_recv,
):
    shot = lax.axis_index("shot")
    domain = lax.axis_index("domain")
    slabs = lax.axis_size("domain")
    rows = pad_p.shape[1] - 2 * PAD
    block = coef.shape[3]
    blocks = coef.shape[0]
    lanes = pad_p.shape[2]
    has_low = domain > 0
    has_high = domain < slabs - 1

    def other(dx, dy):
        return lax.rem(shot // 2 + dx, 4) * 2 + lax.rem(lax.rem(shot, 2) + dy, 2)

    def step_of(place):
        dx = jnp.where(
            (place == 2) | (place == 4), 1, jnp.where((place == 3) | (place == 5), 3, jnp.where(place >= 6, 2, 0))
        )
        dy = jnp.where((place == 1) | (place == 4) | (place == 5) | (place == 7), 1, 0)
        return other(dx, dy)

    locals_ = []

    def local(src, dst):
        copy = pltpu.make_async_copy(src, dst, local_sem.at[len(locals_)])
        copy.start()
        locals_.append(copy)

    for place, field in enumerate((velsq, epsilon, delta, tilt, azimuth)):
        local(field, coef.at[shot, place])
    inside = pl.ds(PAD, rows)
    for pad, state, place in ((pad_p, forward, 1), (pad_q, forward, 3), (pad_a, adjoint, 1), (pad_b, adjoint, 3)):
        local(state.at[0, place], pad.at[pl.ds(1, 2), inside])
    for place, (state, member) in enumerate(((forward, 0), (forward, 2), (adjoint, 0), (adjoint, 2))):
        local(state.at[0, member], olds.at[place])

    barrier = pltpu.get_barrier_semaphore()
    for dx, dy in PEERS:
        pl.semaphore_signal(barrier, inc=1, device_id=(other(dx, dy), domain), device_id_type=MESH)

    @pl.when(has_low)
    def _():
        pl.semaphore_signal(barrier, inc=1, device_id=(shot, domain - 1), device_id_type=MESH)

    @pl.when(has_high)
    def _():
        pl.semaphore_signal(barrier, inc=1, device_id=(shot, domain + 1), device_id_type=MESH)

    for pad in (pad_p, pad_q, pad_a, pad_b, pad_p1, pad_q1):
        zero = jnp.zeros((4, PAD, lanes), jnp.float32)
        pad[:, 0:PAD, :] = zero
        pad[:, PAD + rows : 2 * PAD + rows, :] = zero

    @pl.when(jnp.logical_not(has_low))
    def _():
        for pad in (pad_p, pad_q, pad_a, pad_b, pad_p1, pad_q1):
            pad[0, PAD : PAD + rows, :] = jnp.zeros((rows, lanes), jnp.float32)

    @pl.when(jnp.logical_not(has_high))
    def _():
        for pad in (pad_p, pad_q, pad_a, pad_b, pad_p1, pad_q1):
            pad[3, PAD : PAD + rows, :] = jnp.zeros((rows, lanes), jnp.float32)

    pl.semaphore_wait(barrier, len(PEERS) + has_low.astype(jnp.int32) + has_high.astype(jnp.int32))

    def halo(src_low, src_high, pad, span, sems_send, sems_recv, low, high):
        down = pltpu.make_async_remote_copy(
            src_ref=src_low,
            dst_ref=pad.at[3, span],
            send_sem=sems_send.at[low],
            recv_sem=sems_recv.at[low],
            device_id=(shot, domain - 1),
            device_id_type=MESH,
        )
        up = pltpu.make_async_remote_copy(
            src_ref=src_high,
            dst_ref=pad.at[0, span],
            send_sem=sems_send.at[high],
            recv_sem=sems_recv.at[high],
            device_id=(shot, domain + 1),
            device_id_type=MESH,
        )
        return down, up

    def begin(pair):
        pl.when(has_low)(pair[0].start)
        pl.when(has_high)(pair[1].start)

    def arrived(pair):
        pl.when(has_high)(pair[0].wait_recv)
        pl.when(has_low)(pair[1].wait_recv)

    def sent(pair):
        pl.when(has_low)(pair[0].wait_send)
        pl.when(has_high)(pair[1].wait_send)

    first_halo = []
    for place, (pad, state, member) in enumerate(
        ((pad_p, forward, 1), (pad_q, forward, 3), (pad_a, adjoint, 1), (pad_b, adjoint, 3))
    ):
        first_halo.append(
            halo(state.at[0, member, 0], state.at[0, member, 1], pad, inside, halo_send, halo_recv, 2 * place, 2 * place + 1)
        )
    begin(first_halo[0])
    begin(first_halo[1])

    for copy in locals_[0:5]:
        copy.wait()

    def gather(place, dx, dy):
        return pltpu.make_async_remote_copy(
            src_ref=coef.at[shot],
            dst_ref=coef.at[shot],
            send_sem=gather_send.at[place],
            recv_sem=gather_recv.at[MIRROR[place]],
            device_id=(other(dx, dy), domain),
            device_id_type=MESH,
        )

    gathers = [gather(place, dx, dy) for place, (dx, dy) in enumerate(PEERS)]
    for copy in gathers:
        copy.start()
    begin(first_halo[2])
    begin(first_halo[3])

    cells = receivers[...] - domain * (2 * rows * lanes)
    at_row = lax.shift_right_arithmetic(cells, 7)
    at_lane = cells & (lanes - 1)
    count = cells.shape[1]
    lane_of = lax.broadcasted_iota(jnp.int32, (lanes, count), 0)
    by_lane = jnp.where(lane_of == at_lane, 1.0, 0.0)
    recorded = by_lane * observed[0, 1:2, :]
    contract = (((1,), (1,)), ((), ()))
    for plane in range(2):
        row_of = lax.broadcasted_iota(jnp.int32, (rows, count), 0) + plane * rows
        by_row = jnp.where(row_of == at_row, 1.0, 0.0)
        hits[0, plane] = lax.dot_general(
            by_row, by_lane, contract, precision=lax.Precision.HIGHEST, preferred_element_type=jnp.float32
        )
        hits[1, plane] = lax.dot_general(
            by_row, recorded, contract, precision=lax.Precision.HIGHEST, preferred_element_type=jnp.float32
        )

    shape = (2, TILE, lanes)
    lane = lax.broadcasted_iota(jnp.int32, shape, 2)
    first = lane == 0
    last = lane == lanes - 1
    cell = lax.broadcasted_iota(jnp.int32, shape, 0) * (rows * lanes) + lax.broadcasted_iota(jnp.int32, shape, 1) * lanes + lane
    source_at = source[0] - domain * (2 * rows * lanes)

    def at_source(row, amount):
        return jnp.where(cell == source_at - row * lanes, amount, 0.0)

    for copy in locals_[5:]:
        copy.wait()
    arrived(first_halo[0])
    arrived(first_halo[1])

    def next_halo(owner):
        span = pl.ds(pl.multiple_of(owner * block + PAD, TILE), block)
        pairs = []
        for place, pad in enumerate((pad_p1, pad_q1)):
            at = (owner * 2 + place) * 2
            pairs.append(halo(pad.at[1, span], pad.at[2, span], pad, span, next_send, next_recv, at, at + 1))
        return pairs

    def forward_tile(owner, tile):
        inner = pl.ds(pl.multiple_of(tile * TILE, TILE), TILE)
        row = pl.multiple_of(owner * block + tile * TILE, TILE)
        span = pl.ds(row, TILE)
        speed, eps, dlt, til, azi = (coef[owner, place, :, inner, :] for place in range(5))
        sin_t, cos_t = sin_cos(til)
        sin_a, cos_a = sin_cos_wide(azi)
        axis = (sin_t * cos_a, sin_t * sin_a, cos_t)
        turn = (cos_t * cos_a, cos_t * sin_a, -sin_t)
        quarter = tuple(0.25 * part for part in axis)
        stretch = 1.0 + 2.0 * eps
        root = jnp.sqrt(1.0 + 2.0 * dlt)
        for place, values in enumerate(axis + turn + (stretch, root, speed)):
            table[place, :, span, :] = values
        here_p, hess_p = hessian(pad_p, row + PAD, first, last)
        here_q, hess_q = hessian(pad_q, row + PAD, first, last)
        lean_p = times_axis(hess_p, axis, quarter)
        lean_q = times_axis(hess_q, axis, quarter)
        across = hess_p[0] + hess_p[1] + hess_p[2] - dot3(axis, lean_p)
        axial = dot3(axis, lean_q)
        drive_p = stretch * across + root * axial
        drive_q = root * across + axial
        pulse = at_source(row, wavelet[0, 0])
        here = pl.ds(pl.multiple_of(row + PAD, TILE), TILE)
        pad_p1[1:3, here, :] = 2.0 * here_p - olds[0, :, span, :] + speed * drive_p + pulse
        pad_q1[1:3, here, :] = 2.0 * here_q - olds[1, :, span, :] + speed * drive_q + pulse
        for place, values in enumerate(
            (
                across,
                axial,
                2.0 * dot3(turn, lean_p),
                2.0 * dot3(turn, lean_q),
                2.0 * (axis[0] * lean_p[1] - axis[1] * lean_p[0]),
                2.0 * (axis[0] * lean_q[1] - axis[1] * lean_q[0]),
            )
        ):
            terms[place, :, span, :] = values

    tiles = block // TILE

    def forward_block(place, carry):
        owner = step_of(place)

        @pl.when(place > 0)
        def _():
            pltpu.make_async_copy(coef.at[owner], coef.at[owner], gather_recv.at[place - 1]).wait()

        lax.fori_loop(0, tiles, lambda tile, c: (forward_tile(owner, tile), c)[1], 0)
        for pair in next_halo(owner):
            begin(pair)
        return carry

    lax.fori_loop(0, blocks, forward_block, 0)

    arrived(first_halo[2])
    arrived(first_halo[3])

    def load_table(span):
        values = tuple(table[place, :, span, :] for place in range(9))
        return values[0:3], values[3:6], values[6], values[7], values[8]

    def adjoint_tile(tile, carry):
        row = pl.multiple_of(tile * TILE, TILE)
        span = pl.ds(row, TILE)
        axis, _, stretch, root, speed = load_table(span)
        quarter = tuple(0.25 * part for part in axis)
        here_a, hess_a = hessian(pad_a, row + PAD, first, last)
        here_b, hess_b = hessian(pad_b, row + PAD, first, last)
        across = hess_a[0] + hess_a[1] + hess_a[2] - dot3(axis, times_axis(hess_a, axis, quarter))
        axial = dot3(axis, times_axis(hess_b, axis, quarter))
        step_a[0, :, span, :] = 2.0 * here_a - olds[2, :, span, :] + speed * (stretch * across + root * axial)
        step_a[1, :, span, :] = 2.0 * here_b - olds[3, :, span, :] + speed * (root * across + axial)
        return carry

    lax.fori_loop(0, rows // TILE, adjoint_tile, 0)

    def halo_in(owner, carry):
        for pair in next_halo(owner):
            arrived(pair)
        return carry

    lax.fori_loop(0, blocks, halo_in, 0)

    def gradient_tile(owner, tile):
        inner = pl.ds(pl.multiple_of(tile * TILE, TILE), TILE)
        row = pl.multiple_of(owner * block + tile * TILE, TILE)
        span = pl.ds(row, TILE)
        axis, turn, stretch, root, speed = load_table(span)
        quarter = tuple(0.25 * part for part in axis)
        here_p, hess_p = hessian(pad_p1, row + PAD, first, last)
        _, hess_q = hessian(pad_q1, row + PAD, first, last)
        lean_p = times_axis(hess_p, axis, quarter)
        lean_q = times_axis(hess_q, axis, quarter)
        across1 = hess_p[0] + hess_p[1] + hess_p[2] - dot3(axis, lean_p)
        axial1 = dot3(axis, lean_q)
        here = pl.ds(pl.multiple_of(row + PAD, TILE), TILE)
        last_p = 2.0 * here_p - pad_p[1:3, here, :] + speed * (stretch * across1 + root * axial1)
        last_p = last_p + at_source(row, wavelet[0, 1])
        late_a, late_b = pad_a[1:3, here, :], pad_b[1:3, here, :]
        early_a = step_a[0, :, span, :] + (hits[0, :, span, :] * last_p - hits[1, :, span, :])
        early_b = step_a[1, :, span, :]
        across0, axial0, tilt_p0, tilt_q0, spin_p0, spin_q0 = (terms[place, :, span, :] for place in range(6))
        tilt_p1 = 2.0 * dot3(turn, lean_p)
        tilt_q1 = 2.0 * dot3(turn, lean_q)
        spin_p1 = 2.0 * (axis[0] * lean_p[1] - axis[1] * lean_p[0])
        spin_q1 = 2.0 * (axis[0] * lean_q[1] - axis[1] * lean_q[0])
        by_stretch = early_a * across0 + late_a * across1
        by_root = early_a * axial0 + early_b * across0 + late_a * axial1 + late_b * across1
        by_one = early_b * axial0 + late_b * axial1

        def turned(p0, q0, p1, q1):
            return speed * (
                root * (early_a * q0 - early_b * p0 + late_a * q1 - late_b * p1)
                - stretch * (early_a * p0 + late_a * p1)
                + (early_b * q0 + late_b * q1)
            )

        for place, values in enumerate(
            (
                stretch * by_stretch + root * by_root + by_one,
                2.0 * speed * by_stretch,
                speed * by_root / root,
                turned(tilt_p0, tilt_q0, tilt_p1, tilt_q1),
                turned(spin_p0, spin_q0, spin_p1, spin_q1),
            )
        ):
            grad[owner, place, :, inner, :] = values

    def summand(place, owner):
        mirror = jnp.where(
            (place == 1) | (place == 3), place + 1, jnp.where((place == 2) | (place == 4), place - 1, place)
        )
        return pltpu.make_async_remote_copy(
            src_ref=grad.at[owner],
            dst_ref=parts.at[mirror],
            send_sem=sum_send.at[place],
            recv_sem=sum_recv.at[mirror],
            device_id=(owner, domain),
            device_id_type=MESH,
        )

    def gradient_block(turn_at, carry):
        place = blocks - 1 - turn_at
        owner = step_of(place)
        lax.fori_loop(0, tiles, lambda tile, c: (gradient_tile(owner, tile), c)[1], 0)

        @pl.when(place > 0)
        def _():
            summand(place - 1, owner).start()

        return carry

    lax.fori_loop(0, blocks, gradient_block, 0)

    def add_part(place, carry):
        summand(place, step_of(place + 1)).wait_recv()
        return carry

    lax.fori_loop(0, blocks - 1, add_part, 0)
    total = grad[shot]
    for place in range(blocks - 1):
        total = total + parts[place]
    out[...] = total

    for copy in gathers:
        copy.wait_send()
    for pair in first_halo:
        sent(pair)

    def drained(owner, carry):
        for pair in next_halo(owner):
            sent(pair)
        return carry

    lax.fori_loop(0, blocks, drained, 0)

    def parts_left(place, carry):
        summand(place, step_of(place + 1)).wait_send()
        return carry

    lax.fori_loop(0, blocks - 1, parts_left, 0)


def shards(velsq, epsilon, delta, tilt, azimuth, forward, adjoint, wavelet, source, receivers, observed):
    planes, block, lanes = velsq.shape
    rows = forward.shape[3]
    blocks = rows // block
    padded = pltpu.VMEM((planes + 2, rows + 2 * PAD, lanes), jnp.float32)
    anywhere = pl.BlockSpec(memory_space=pl.ANY)
    vmem = pl.BlockSpec(memory_space=pltpu.VMEM)
    smem = pl.BlockSpec(memory_space=pltpu.SMEM)

    def fields(*lead):
        return pltpu.VMEM(lead + (planes, rows, lanes), jnp.float32)

    def by_block(count):
        return pltpu.VMEM((count, 5, planes, block, lanes), jnp.float32)

    sems = pltpu.SemaphoreType.DMA
    return pl.pallas_call(
        kernel,
        out_shape=jax.ShapeDtypeStruct((5, planes, block, lanes), jnp.float32),
        in_specs=[anywhere] * 7 + [smem, smem, vmem, vmem],
        out_specs=vmem,
        scratch_shapes=[by_block(blocks)]
        + [padded] * 6
        + [fields(4), fields(9), fields(6), fields(2), fields(2), by_block(blocks), by_block(blocks - 1)]
        + [
            sems((13,)),
            sems((blocks - 1,)),
            sems((blocks - 1,)),
            sems((8,)),
            sems((8,)),
            sems((4 * blocks,)),
            sems((4 * blocks,)),
            sems((blocks - 1,)),
            sems((blocks - 1,)),
        ],
        compiler_params=pltpu.CompilerParams(
            collective_id=0, has_side_effects=True, vmem_limit_bytes=40 << 20
        ),
        name="gradient",
    )(velsq, epsilon, delta, tilt, azimuth, forward, adjoint, wavelet, source, receivers, observed)


def solution(mesh):
    field = P("domain", "shot", None)
    state = P("shot", None, "domain", None, None)
    return jax.shard_map(
        shards,
        mesh=mesh,
        in_specs=(field,) * 5 + (state, state, P("shot", None), P("shot"), P("shot", None), P("shot", None, None)),
        out_specs=P(None, "domain", "shot", None),
        check_vma=False,
    )
```

```python
import functools

import jax
import jax.numpy as jnp
from jax import lax
from jax.experimental import pallas as pl
from jax.experimental.pallas import tpu as pltpu
from jax.sharding import PartitionSpec as P

MESH = pl.DeviceIdType.MESH
TILE = 8
PAD = 8


SIN = (1.0, -1 / 6, 1 / 120, -1 / 5040, 1 / 362880, -1 / 39916800, 1 / 6227020800)
COS = (1.0, -1 / 2, 1 / 24, -1 / 720, 1 / 40320, -1 / 3628800, 1 / 479001600, -1 / 87178291200)


def horner(square, series):
    total = jnp.float32(series[-1])
    for term in series[-2::-1]:
        total = total * square + jnp.float32(term)
    return total


def sin_cos(angle):
    square = angle * angle
    return angle * horner(square, SIN), horner(square, COS)


def sin_cos_wide(angle):
    half_sin, half_cos = sin_cos(0.5 * angle)
    return 2.0 * half_sin * half_cos, 1.0 - 2.0 * half_sin * half_sin


def hessian(pad_ref, row, first, last):
    here = pad_ref[:, pl.ds(row, TILE), :]
    above = pad_ref[:, pl.ds(row + 1, TILE), :]
    below = pad_ref[:, pl.ds(row - 1, TILE), :]

    def ahead(values):
        return jnp.where(last, 0.0, pltpu.roll(values, values.shape[-1] - 1, 2))

    def behind(values):
        return jnp.where(first, 0.0, pltpu.roll(values, 1, 2))

    center = here[1:3]
    twice = 2.0 * center
    along_x = here[2:4] - here[0:2]
    along_y = above[1:3] - below[1:3]
    xx = here[2:4] + here[0:2] - twice
    yy = above[1:3] + below[1:3] - twice
    zz = ahead(center) + behind(center) - twice
    xy = (above[2:4] - above[0:2]) - (below[2:4] - below[0:2])
    xz = ahead(along_x) - behind(along_x)
    yz = ahead(along_y) - behind(along_y)
    return center, (xx, yy, zz, xy, xz, yz)


def times_axis(parts, axis, quarter):
    xx, yy, zz, xy, xz, yz = parts
    return (
        xx * axis[0] + xy * quarter[1] + xz * quarter[2],
        xy * quarter[0] + yy * axis[1] + yz * quarter[2],
        xz * quarter[0] + yz * quarter[1] + zz * axis[2],
    )


def dot3(left, right):
    return left[0] * right[0] + left[1] * right[1] + left[2] * right[2]


def kernel(
    velsq,
    epsilon,
    delta,
    tilt,
    azimuth,
    forward,
    adjoint,
    wavelet,
    source,
    receivers,
    observed,
    out,
    coef,
    pad_p,
    pad_q,
    pad_a,
    pad_b,
    pad_p1,
    pad_q1,
    olds,
    table,
    terms,
    step_a,
    hits,
    grad,
    far,
    near,
    mates,
    local_sem,
    gather_send,
    gather_recv,
    halo_send,
    halo_recv,
    next_send,
    next_recv,
    far_send,
    far_recv,
    near_send,
    near_recv,
    mate_send,
    mate_recv,
):
    shot = lax.axis_index("shot")
    domain = lax.axis_index("domain")
    slabs = lax.axis_size("domain")
    rows = pad_p.shape[1] - 2 * PAD
    block = coef.shape[3]
    blocks = coef.shape[0]
    lanes = pad_p.shape[2]
    has_low = domain > 0
    has_high = domain < slabs - 1

    def other(dx, dy):
        return lax.rem(shot // 2 + dx, 4) * 2 + lax.rem(lax.rem(shot, 2) + dy, 2)

    def step_of(place):
        dx = jnp.where(
            (place == 2) | (place == 4), 1, jnp.where((place == 3) | (place == 5), 3, jnp.where(place >= 6, 2, 0))
        )
        dy = jnp.where((place == 1) | (place == 4) | (place == 5) | (place == 7), 1, 0)
        return other(dx, dy)

    locals_ = []

    def local(src, dst):
        copy = pltpu.make_async_copy(src, dst, local_sem.at[len(locals_)])
        copy.start()
        locals_.append(copy)

    for place, field in enumerate((velsq, epsilon, delta, tilt, azimuth)):
        local(field, coef.at[shot, :, place])
    inside = pl.ds(PAD, rows)
    for pad, state, place in ((pad_p, forward, 1), (pad_q, forward, 3), (pad_a, adjoint, 1), (pad_b, adjoint, 3)):
        local(state.at[0, place], pad.at[pl.ds(1, 2), inside])
    for place, (state, member) in enumerate(((forward, 0), (forward, 2), (adjoint, 0), (adjoint, 2))):
        local(state.at[0, member], olds.at[place])

    barrier = pltpu.get_barrier_semaphore()
    mate, right, left = other(0, 1), other(1, 0), other(3, 0)
    for peer in (mate, right, left):
        pl.semaphore_signal(barrier, inc=1, device_id=(peer, domain), device_id_type=MESH)

    @pl.when(has_low)
    def _():
        pl.semaphore_signal(barrier, inc=1, device_id=(shot, domain - 1), device_id_type=MESH)

    @pl.when(has_high)
    def _():
        pl.semaphore_signal(barrier, inc=1, device_id=(shot, domain + 1), device_id_type=MESH)

    for pad in (pad_p, pad_q, pad_a, pad_b, pad_p1, pad_q1):
        zero = jnp.zeros((4, PAD, lanes), jnp.float32)
        pad[:, 0:PAD, :] = zero
        pad[:, PAD + rows : 2 * PAD + rows, :] = zero

    @pl.when(jnp.logical_not(has_low))
    def _():
        for pad in (pad_p, pad_q, pad_a, pad_b, pad_p1, pad_q1):
            pad[0, PAD : PAD + rows, :] = jnp.zeros((rows, lanes), jnp.float32)

    @pl.when(jnp.logical_not(has_high))
    def _():
        for pad in (pad_p, pad_q, pad_a, pad_b, pad_p1, pad_q1):
            pad[3, PAD : PAD + rows, :] = jnp.zeros((rows, lanes), jnp.float32)

    pl.semaphore_wait(barrier, 3 + has_low.astype(jnp.int32) + has_high.astype(jnp.int32))

    def halo(src_low, src_high, pad, span, sems_send, sems_recv, low, high):
        down = pltpu.make_async_remote_copy(
            src_ref=src_low,
            dst_ref=pad.at[3, span],
            send_sem=sems_send.at[low],
            recv_sem=sems_recv.at[low],
            device_id=(shot, domain - 1),
            device_id_type=MESH,
        )
        up = pltpu.make_async_remote_copy(
            src_ref=src_high,
            dst_ref=pad.at[0, span],
            send_sem=sems_send.at[high],
            recv_sem=sems_recv.at[high],
            device_id=(shot, domain + 1),
            device_id_type=MESH,
        )
        return down, up

    def begin(pair):
        pl.when(has_low)(pair[0].start)
        pl.when(has_high)(pair[1].start)

    def arrived(pair):
        pl.when(has_high)(pair[0].wait_recv)
        pl.when(has_low)(pair[1].wait_recv)

    def sent(pair):
        pl.when(has_low)(pair[0].wait_send)
        pl.when(has_high)(pair[1].wait_send)

    first_halo = []
    for place, (pad, state, member) in enumerate(
        ((pad_p, forward, 1), (pad_q, forward, 3), (pad_a, adjoint, 1), (pad_b, adjoint, 3))
    ):
        first_halo.append(
            halo(state.at[0, member, 0], state.at[0, member, 1], pad, inside, halo_send, halo_recv, 2 * place, 2 * place + 1)
        )
    def push(part, peer, send_sem, recv_sem):
        return pltpu.make_async_remote_copy(
            src_ref=part,
            dst_ref=part,
            send_sem=send_sem,
            recv_sem=recv_sem,
            device_id=(peer, domain),
            device_id_type=MESH,
        )

    def landed(part, recv_sem):
        pltpu.make_async_copy(part, part, recv_sem).wait()

    sends = [
        push(coef.at[shot], mate, gather_send.at[0], gather_recv.at[1]),
        push(coef.at[shot], right, gather_send.at[1], gather_recv.at[3]),
        push(coef.at[shot], left, gather_send.at[2], gather_recv.at[2]),
        push(coef.at[mate], right, gather_send.at[3], gather_recv.at[5]),
        push(coef.at[mate], left, gather_send.at[4], gather_recv.at[4]),
        push(coef.at[left, 0], right, gather_send.at[5], gather_recv.at[6]),
        push(coef.at[right, 1], left, gather_send.at[6], gather_recv.at[7]),
        push(coef.at[other(3, 1), 0], right, gather_send.at[7], gather_recv.at[8]),
        push(coef.at[other(1, 1), 1], left, gather_send.at[8], gather_recv.at[9]),
    ]
    for copy in locals_[0:5]:
        copy.wait()
    for copy in sends[0:3]:
        copy.start()
    begin(first_halo[0])
    begin(first_halo[1])

    cells = receivers[...] - domain * (2 * rows * lanes)
    at_row = lax.shift_right_arithmetic(cells, 7)
    at_lane = cells & (lanes - 1)
    count = cells.shape[1]
    lane_of = lax.broadcasted_iota(jnp.int32, (lanes, count), 0)
    by_lane = jnp.where(lane_of == at_lane, 1.0, 0.0)
    recorded = by_lane * observed[0, 1:2, :]
    contract = (((1,), (1,)), ((), ()))
    for plane in range(2):
        row_of = lax.broadcasted_iota(jnp.int32, (rows, count), 0) + plane * rows
        by_row = jnp.where(row_of == at_row, 1.0, 0.0)
        hits[0, plane] = lax.dot_general(
            by_row, by_lane, contract, precision=lax.Precision.HIGHEST, preferred_element_type=jnp.float32
        )
        hits[1, plane] = lax.dot_general(
            by_row, recorded, contract, precision=lax.Precision.HIGHEST, preferred_element_type=jnp.float32
        )

    shape = (2, TILE, lanes)
    lane = lax.broadcasted_iota(jnp.int32, shape, 2)
    first = lane == 0
    last = lane == lanes - 1
    cell = lax.broadcasted_iota(jnp.int32, shape, 0) * (rows * lanes) + lax.broadcasted_iota(jnp.int32, shape, 1) * lanes + lane
    source_at = source[0] - domain * (2 * rows * lanes)

    def at_source(row, amount):
        return jnp.where(cell == source_at - row * lanes, amount, 0.0)

    landed(coef.at[mate], gather_recv.at[1])
    sends[3].start()
    sends[4].start()
    landed(coef.at[left], gather_recv.at[3])
    sends[5].start()
    landed(coef.at[right], gather_recv.at[2])
    sends[6].start()
    begin(first_halo[2])
    begin(first_halo[3])
    for copy in locals_[5:]:
        copy.wait()
    arrived(first_halo[0])
    arrived(first_halo[1])

    def next_halo(owner):
        span = pl.ds(pl.multiple_of(owner * block + PAD, TILE), block)
        pairs = []
        for place, pad in enumerate((pad_p1, pad_q1)):
            at = (owner * 2 + place) * 2
            pairs.append(halo(pad.at[1, span], pad.at[2, span], pad, span, next_send, next_recv, at, at + 1))
        return pairs

    def forward_tile(owner, tile):
        inner = pl.ds(pl.multiple_of(tile * TILE, TILE), TILE)
        row = pl.multiple_of(owner * block + tile * TILE, TILE)
        span = pl.ds(row, TILE)
        speed, eps, dlt, til, azi = (coef[owner, :, place, inner, :] for place in range(5))
        sin_t, cos_t = sin_cos(til)
        sin_a, cos_a = sin_cos_wide(azi)
        axis = (sin_t * cos_a, sin_t * sin_a, cos_t)
        turn = (cos_t * cos_a, cos_t * sin_a, -sin_t)
        quarter = tuple(0.25 * part for part in axis)
        stretch = 1.0 + 2.0 * eps
        root = jnp.sqrt(1.0 + 2.0 * dlt)
        for place, values in enumerate(axis + turn + (stretch, root, speed)):
            table[place, :, span, :] = values
        here_p, hess_p = hessian(pad_p, row + PAD, first, last)
        here_q, hess_q = hessian(pad_q, row + PAD, first, last)
        lean_p = times_axis(hess_p, axis, quarter)
        lean_q = times_axis(hess_q, axis, quarter)
        across = hess_p[0] + hess_p[1] + hess_p[2] - dot3(axis, lean_p)
        axial = dot3(axis, lean_q)
        drive_p = stretch * across + root * axial
        drive_q = root * across + axial
        pulse = at_source(row, wavelet[0, 0])
        here = pl.ds(pl.multiple_of(row + PAD, TILE), TILE)
        pad_p1[1:3, here, :] = 2.0 * here_p - olds[0, :, span, :] + speed * drive_p + pulse
        pad_q1[1:3, here, :] = 2.0 * here_q - olds[1, :, span, :] + speed * drive_q + pulse
        for place, values in enumerate(
            (
                across,
                axial,
                2.0 * dot3(turn, lean_p),
                2.0 * dot3(turn, lean_q),
                2.0 * (axis[0] * lean_p[1] - axis[1] * lean_p[0]),
                2.0 * (axis[0] * lean_q[1] - axis[1] * lean_q[0]),
            )
        ):
            terms[place, :, span, :] = values

    tiles = block // TILE

    def forward_block(place, carry):
        owner = step_of(place)

        @pl.when(place == 3)
        def _():
            landed(coef.at[other(3, 1)], gather_recv.at[5])
            sends[7].start()
            landed(coef.at[other(1, 1)], gather_recv.at[4])
            sends[8].start()

        @pl.when(place >= 6)
        def _():
            for plane in range(2):
                landed(coef.at[owner, plane], gather_recv.at[2 * place - 6 + plane])

        lax.fori_loop(0, tiles, lambda tile, c: (forward_tile(owner, tile), c)[1], 0)
        for pair in next_halo(owner):
            begin(pair)
        return carry

    lax.fori_loop(0, blocks, forward_block, 0)

    arrived(first_halo[2])
    arrived(first_halo[3])

    def load_table(span):
        values = tuple(table[place, :, span, :] for place in range(9))
        return values[0:3], values[3:6], values[6], values[7], values[8]

    def adjoint_tile(tile, carry):
        row = pl.multiple_of(tile * TILE, TILE)
        span = pl.ds(row, TILE)
        axis, _, stretch, root, speed = load_table(span)
        quarter = tuple(0.25 * part for part in axis)
        here_a, hess_a = hessian(pad_a, row + PAD, first, last)
        here_b, hess_b = hessian(pad_b, row + PAD, first, last)
        across = hess_a[0] + hess_a[1] + hess_a[2] - dot3(axis, times_axis(hess_a, axis, quarter))
        axial = dot3(axis, times_axis(hess_b, axis, quarter))
        step_a[0, :, span, :] = 2.0 * here_a - olds[2, :, span, :] + speed * (stretch * across + root * axial)
        step_a[1, :, span, :] = 2.0 * here_b - olds[3, :, span, :] + speed * (root * across + axial)
        return carry

    lax.fori_loop(0, rows // TILE, adjoint_tile, 0)

    def halo_in(owner, carry):
        for pair in next_halo(owner):
            arrived(pair)
        return carry

    lax.fori_loop(0, blocks, halo_in, 0)

    def gradient_tile(owner, tile):
        inner = pl.ds(pl.multiple_of(tile * TILE, TILE), TILE)
        row = pl.multiple_of(owner * block + tile * TILE, TILE)
        span = pl.ds(row, TILE)
        axis, turn, stretch, root, speed = load_table(span)
        quarter = tuple(0.25 * part for part in axis)
        here_p, hess_p = hessian(pad_p1, row + PAD, first, last)
        _, hess_q = hessian(pad_q1, row + PAD, first, last)
        lean_p = times_axis(hess_p, axis, quarter)
        lean_q = times_axis(hess_q, axis, quarter)
        across1 = hess_p[0] + hess_p[1] + hess_p[2] - dot3(axis, lean_p)
        axial1 = dot3(axis, lean_q)
        here = pl.ds(pl.multiple_of(row + PAD, TILE), TILE)
        last_p = 2.0 * here_p - pad_p[1:3, here, :] + speed * (stretch * across1 + root * axial1)
        last_p = last_p + at_source(row, wavelet[0, 1])
        late_a, late_b = pad_a[1:3, here, :], pad_b[1:3, here, :]
        early_a = step_a[0, :, span, :] + (hits[0, :, span, :] * last_p - hits[1, :, span, :])
        early_b = step_a[1, :, span, :]
        across0, axial0, tilt_p0, tilt_q0, spin_p0, spin_q0 = (terms[place, :, span, :] for place in range(6))
        tilt_p1 = 2.0 * dot3(turn, lean_p)
        tilt_q1 = 2.0 * dot3(turn, lean_q)
        spin_p1 = 2.0 * (axis[0] * lean_p[1] - axis[1] * lean_p[0])
        spin_q1 = 2.0 * (axis[0] * lean_q[1] - axis[1] * lean_q[0])
        by_stretch = early_a * across0 + late_a * across1
        by_root = early_a * axial0 + early_b * across0 + late_a * axial1 + late_b * across1
        by_one = early_b * axial0 + late_b * axial1

        def turned(p0, q0, p1, q1):
            return speed * (
                root * (early_a * q0 - early_b * p0 + late_a * q1 - late_b * p1)
                - stretch * (early_a * p0 + late_a * p1)
                + (early_b * q0 + late_b * q1)
            )

        for place, values in enumerate(
            (
                stretch * by_stretch + root * by_root + by_one,
                2.0 * speed * by_stretch,
                speed * by_root / root,
                turned(tilt_p0, tilt_q0, tilt_p1, tilt_q1),
                turned(spin_p0, spin_q0, spin_p1, spin_q1),
            )
        ):
            grad[owner, :, place, inner, :] = values

    def far_part(side, where):
        return pltpu.make_async_remote_copy(
            src_ref=grad.at[other(2, where), side],
            dst_ref=far.at[side, where],
            send_sem=far_send.at[2 * side + where],
            recv_sem=far_recv.at[2 * side + where],
            device_id=((right, left)[side], domain),
            device_id_type=MESH,
        )

    def near_part(side, where):
        return pltpu.make_async_remote_copy(
            src_ref=grad.at[other((1, 3)[side], where)],
            dst_ref=near.at[side, where],
            send_sem=near_send.at[2 * side + where],
            recv_sem=near_recv.at[2 * side + where],
            device_id=((right, left)[side], domain),
            device_id_type=MESH,
        )

    def pass_sums(where):
        for side in range(2):
            owner = other((1, 3)[side], where)
            far_part(side, where).wait_recv()
            grad[owner, side] = grad[owner, side] + far[side, where]
            near_part(side, where).start()

    def gradient_block(turn_at, carry):
        place = jnp.where(
            turn_at < 2,
            7 - turn_at,
            jnp.where(turn_at < 4, turn_at + 2, jnp.where(turn_at < 6, turn_at - 2, 7 - turn_at)),
        )
        owner = step_of(place)
        lax.fori_loop(0, tiles, lambda tile, c: (gradient_tile(owner, tile), c)[1], 0)
        for where in range(2):

            @pl.when(turn_at == 1 - where)
            def _():
                for side in range(2):
                    far_part(side, where).start()

            @pl.when(turn_at == 5 - 2 * where)
            def _():
                pass_sums(where)

        return carry

    lax.fori_loop(0, blocks, gradient_block, 0)

    swap = pltpu.make_async_remote_copy(
        src_ref=grad.at[mate],
        dst_ref=mates,
        send_sem=mate_send,
        recv_sem=mate_recv,
        device_id=(mate, domain),
        device_id_type=MESH,
    )
    for side in range(2):
        near_part(side, 1).wait_recv()
    grad[mate] = grad[mate] + (near[0, 1] + near[1, 1])
    swap.start()
    for side in range(2):
        near_part(side, 0).wait_recv()
    total = grad[shot] + (near[0, 0] + near[1, 0])
    swap.wait_recv()
    total = total + mates[...]
    for plane in range(2):
        out[:, plane] = total[plane]

    for copy in sends:
        copy.wait_send()
    for pair in first_halo:
        sent(pair)

    def drained(owner, carry):
        for pair in next_halo(owner):
            sent(pair)
        return carry

    lax.fori_loop(0, blocks, drained, 0)
    for side in range(2):
        for where in range(2):
            far_part(side, where).wait_send()
            near_part(side, where).wait_send()
    swap.wait_send()


def shards(velsq, epsilon, delta, tilt, azimuth, forward, adjoint, wavelet, source, receivers, observed):
    planes, block, lanes = velsq.shape
    rows = forward.shape[3]
    blocks = rows // block
    padded = pltpu.VMEM((planes + 2, rows + 2 * PAD, lanes), jnp.float32)
    anywhere = pl.BlockSpec(memory_space=pl.ANY)
    vmem = pl.BlockSpec(memory_space=pltpu.VMEM)
    smem = pl.BlockSpec(memory_space=pltpu.SMEM)

    def fields(*lead):
        return pltpu.VMEM(lead + (planes, rows, lanes), jnp.float32)

    def by_block(count):
        return pltpu.VMEM(count + (planes, 5, block, lanes), jnp.float32)

    sems = pltpu.SemaphoreType.DMA
    return pl.pallas_call(
        kernel,
        out_shape=jax.ShapeDtypeStruct((5, planes, block, lanes), jnp.float32),
        in_specs=[anywhere] * 7 + [smem, smem, vmem, vmem],
        out_specs=vmem,
        scratch_shapes=[by_block((blocks,))]
        + [padded] * 6
        + [fields(4), fields(9), fields(6), fields(2), fields(2), by_block((blocks,))]
        + [pltpu.VMEM((2, 2, 5, block, lanes), jnp.float32), by_block((2, 2)), by_block(())]
        + [
            sems((13,)),
            sems((9,)),
            sems((10,)),
            sems((8,)),
            sems((8,)),
            sems((4 * blocks,)),
            sems((4 * blocks,)),
            sems((4,)),
            sems((4,)),
            sems((4,)),
            sems((4,)),
            sems(()),
            sems(()),
        ],
        compiler_params=pltpu.CompilerParams(
            collective_id=0, has_side_effects=True, vmem_limit_bytes=60 << 20
        ),
        name="gradient",
    )(velsq, epsilon, delta, tilt, azimuth, forward, adjoint, wavelet, source, receivers, observed)


def solution(mesh):
    field = P("domain", "shot", None)
    state = P("shot", None, "domain", None, None)
    return jax.shard_map(
        shards,
        mesh=mesh,
        in_specs=(field,) * 5 + (state, state, P("shot", None), P("shot"), P("shot", None), P("shot", None, None)),
        out_specs=P(None, "domain", "shot", None),
        check_vma=False,
    )
```

```python
import functools

import jax
import jax.numpy as jnp
from jax import lax
from jax.experimental import pallas as pl
from jax.experimental.pallas import tpu as pltpu
from jax.sharding import PartitionSpec as P

MESH = pl.DeviceIdType.MESH
TILE = 8
PAD = 8


SIN = (1.0, -1 / 6, 1 / 120, -1 / 5040, 1 / 362880, -1 / 39916800, 1 / 6227020800)
COS = (1.0, -1 / 2, 1 / 24, -1 / 720, 1 / 40320, -1 / 3628800, 1 / 479001600, -1 / 87178291200)


def horner(square, series):
    total = jnp.float32(series[-1])
    for term in series[-2::-1]:
        total = total * square + jnp.float32(term)
    return total


def sin_cos(angle):
    square = angle * angle
    return angle * horner(square, SIN), horner(square, COS)


def sin_cos_wide(angle):
    half_sin, half_cos = sin_cos(0.5 * angle)
    return 2.0 * half_sin * half_cos, 1.0 - 2.0 * half_sin * half_sin


def hessian(pad_ref, row, first, last):
    here = pad_ref[:, pl.ds(row, TILE), :]
    above = pad_ref[:, pl.ds(row + 1, TILE), :]
    below = pad_ref[:, pl.ds(row - 1, TILE), :]

    def ahead(values):
        return jnp.where(last, 0.0, pltpu.roll(values, values.shape[-1] - 1, 2))

    def behind(values):
        return jnp.where(first, 0.0, pltpu.roll(values, 1, 2))

    center = here[1:3]
    twice = 2.0 * center
    along_x = here[2:4] - here[0:2]
    along_y = above[1:3] - below[1:3]
    xx = here[2:4] + here[0:2] - twice
    yy = above[1:3] + below[1:3] - twice
    zz = ahead(center) + behind(center) - twice
    xy = (above[2:4] - above[0:2]) - (below[2:4] - below[0:2])
    xz = ahead(along_x) - behind(along_x)
    yz = ahead(along_y) - behind(along_y)
    return center, (xx, yy, zz, xy, xz, yz)


def times_axis(parts, axis, quarter):
    xx, yy, zz, xy, xz, yz = parts
    return (
        xx * axis[0] + xy * quarter[1] + xz * quarter[2],
        xy * quarter[0] + yy * axis[1] + yz * quarter[2],
        xz * quarter[0] + yz * quarter[1] + zz * axis[2],
    )


def dot3(left, right):
    return left[0] * right[0] + left[1] * right[1] + left[2] * right[2]


def kernel(
    velsq,
    epsilon,
    delta,
    tilt,
    azimuth,
    forward,
    adjoint,
    wavelet_in,
    source,
    receivers_in,
    observed_in,
    out,
    wavelet,
    receivers,
    observed,
    coef,
    pad_pq,
    pad_ab,
    pad_next,
    olds,
    table,
    terms,
    step_a,
    hits,
    grad,
    far,
    near,
    mates,
    local_sem,
    gather_send,
    gather_recv,
    halo_send,
    halo_recv,
    next_send,
    next_recv,
    far_send,
    far_recv,
    near_send,
    near_recv,
    mate_send,
    mate_recv,
):
    shot = lax.axis_index("shot")
    domain = lax.axis_index("domain")
    slabs = lax.axis_size("domain")
    rows = pad_pq.shape[2] - 2 * PAD
    block = coef.shape[3]
    blocks = coef.shape[0]
    lanes = pad_pq.shape[3]
    has_low = domain > 0
    has_high = domain < slabs - 1

    def other(dx, dy):
        return lax.rem(shot // 2 + dx, 4) * 2 + lax.rem(lax.rem(shot, 2) + dy, 2)

    def step_of(place):
        dx = jnp.where(
            (place == 2) | (place == 4), 1, jnp.where((place == 3) | (place == 5), 3, jnp.where(place >= 6, 2, 0))
        )
        dy = jnp.where((place == 1) | (place == 4) | (place == 5) | (place == 7), 1, 0)
        return other(dx, dy)

    locals_ = []

    def local(src, dst):
        copy = pltpu.make_async_copy(src, dst, local_sem.at[len(locals_)])
        copy.start()
        locals_.append(copy)

    for place, field in enumerate((velsq, epsilon, delta, tilt, azimuth)):
        local(field, coef.at[shot, :, place])
    inside = pl.ds(PAD, rows)
    for pad, state in ((pad_pq, forward), (pad_ab, adjoint)):
        for place in range(2):
            local(state.at[0, 2 * place + 1], pad.at[place, pl.ds(1, 2), inside])
    for place, (state, member) in enumerate(((forward, 0), (forward, 2), (adjoint, 0), (adjoint, 2))):
        local(state.at[0, member], olds.at[place])

    for src, dst in ((wavelet_in, wavelet), (receivers_in, receivers), (observed_in, observed)):
        local(src, dst)

    barrier = pltpu.get_barrier_semaphore()
    mate, right, left = other(0, 1), other(1, 0), other(3, 0)
    for peer in (mate, right, left):
        pl.semaphore_signal(barrier, inc=1, device_id=(peer, domain), device_id_type=MESH)

    @pl.when(has_low)
    def _():
        pl.semaphore_signal(barrier, inc=1, device_id=(shot, domain - 1), device_id_type=MESH)

    @pl.when(has_high)
    def _():
        pl.semaphore_signal(barrier, inc=1, device_id=(shot, domain + 1), device_id_type=MESH)

    pads = (pad_pq, pad_ab, pad_next)
    for pad in pads:
        zero = jnp.zeros((2, 4, PAD, lanes), jnp.float32)
        pad[:, :, 0:PAD, :] = zero
        pad[:, :, PAD + rows : 2 * PAD + rows, :] = zero

    @pl.when(jnp.logical_not(has_low))
    def _():
        for pad in pads:
            pad[:, 0, PAD : PAD + rows, :] = jnp.zeros((2, rows, lanes), jnp.float32)

    @pl.when(jnp.logical_not(has_high))
    def _():
        for pad in pads:
            pad[:, 3, PAD : PAD + rows, :] = jnp.zeros((2, rows, lanes), jnp.float32)

    pl.semaphore_wait(barrier, 3 + has_low.astype(jnp.int32) + has_high.astype(jnp.int32))

    def halo(pad, span, send, recv, at):
        down = pltpu.make_async_remote_copy(
            src_ref=pad.at[:, 1, span],
            dst_ref=pad.at[:, 3, span],
            send_sem=send.at[at, 0],
            recv_sem=recv.at[at, 0],
            device_id=(shot, domain - 1),
            device_id_type=MESH,
        )
        up = pltpu.make_async_remote_copy(
            src_ref=pad.at[:, 2, span],
            dst_ref=pad.at[:, 0, span],
            send_sem=send.at[at, 1],
            recv_sem=recv.at[at, 1],
            device_id=(shot, domain + 1),
            device_id_type=MESH,
        )
        return down, up

    def begin(pair):
        pl.when(has_low)(pair[0].start)
        pl.when(has_high)(pair[1].start)

    def arrived(pair):
        pl.when(has_high)(pair[0].wait_recv)
        pl.when(has_low)(pair[1].wait_recv)

    def sent(pair):
        pl.when(has_low)(pair[0].wait_send)
        pl.when(has_high)(pair[1].wait_send)

    halo_pq = halo(pad_pq, inside, halo_send, halo_recv, 0)
    halo_ab = halo(pad_ab, inside, halo_send, halo_recv, 1)

    def push(part, peer, send_sem, recv_sem):
        return pltpu.make_async_remote_copy(
            src_ref=part,
            dst_ref=part,
            send_sem=send_sem,
            recv_sem=recv_sem,
            device_id=(peer, domain),
            device_id_type=MESH,
        )

    def landed(part, recv_sem):
        pltpu.make_async_copy(part, part, recv_sem).wait()

    def own_part(plane, side):
        return push(coef.at[shot, plane], (mate, right, left)[side], gather_send.at[3 * plane + side], gather_recv.at[plane, (1, 3, 2)[side]])

    def mate_part(plane, side):
        return push(coef.at[mate, plane], (right, left)[side], gather_send.at[6 + 2 * plane + side], gather_recv.at[plane, (5, 4)[side]])

    def far_coef(where, side):
        part = coef.at[other((3, 1)[side], where), side]
        return push(part, (right, left)[side], gather_send.at[10 + 2 * where + side], gather_recv.at[side, 6 + where])

    def pass_far(where):
        for side in range(2):
            owner = other((3, 1)[side], where)
            landed(coef.at[owner, side], gather_recv.at[side, (3, 2)[side] + 2 * where])
            far_coef(where, side).start()

    for copy in locals_[0:5]:
        copy.wait()
    for plane, side in ((0, 0), (0, 1), (1, 2), (1, 0), (1, 1), (0, 2)):
        own_part(plane, side).start()
    for copy in locals_[5:9]:
        copy.wait()
    begin(halo_pq)
    for copy in locals_[13:]:
        copy.wait()

    cells = receivers[...] - domain * (2 * rows * lanes)
    at_row = lax.shift_right_arithmetic(cells, 7)
    at_lane = cells & (lanes - 1)
    count = cells.shape[1]
    lane_of = lax.broadcasted_iota(jnp.int32, (lanes, count), 0)
    by_lane = jnp.where(lane_of == at_lane, 1.0, 0.0)
    recorded = by_lane * observed[0, 1:2, :]
    contract = (((1,), (1,)), ((), ()))
    for plane in range(2):
        row_of = lax.broadcasted_iota(jnp.int32, (rows, count), 0) + plane * rows
        by_row = jnp.where(row_of == at_row, 1.0, 0.0)
        hits[0, plane] = lax.dot_general(
            by_row, by_lane, contract, precision=lax.Precision.HIGHEST, preferred_element_type=jnp.float32
        )
        hits[1, plane] = lax.dot_general(
            by_row, recorded, contract, precision=lax.Precision.HIGHEST, preferred_element_type=jnp.float32
        )

    shape = (2, TILE, lanes)
    lane = lax.broadcasted_iota(jnp.int32, shape, 2)
    first = lane == 0
    last = lane == lanes - 1
    cell = lax.broadcasted_iota(jnp.int32, shape, 0) * (rows * lanes) + lax.broadcasted_iota(jnp.int32, shape, 1) * lanes + lane
    source_at = source[0] - domain * (2 * rows * lanes)

    def at_source(row, amount):
        return jnp.where(cell == source_at - row * lanes, amount, 0.0)

    for plane in range(2):
        landed(coef.at[mate, plane], gather_recv.at[plane, 1])
        mate_part(plane, plane).start()
        mate_part(plane, 1 - plane).start()
    pass_far(0)
    begin(halo_ab)
    for copy in locals_[9:13]:
        copy.wait()
    arrived(halo_pq)

    def next_halo(owner):
        span = pl.ds(pl.multiple_of(owner * block + PAD, TILE), block)
        return halo(pad_next, span, next_send, next_recv, owner)

    def forward_tile(owner, tile):
        inner = pl.ds(pl.multiple_of(tile * TILE, TILE), TILE)
        row = pl.multiple_of(owner * block + tile * TILE, TILE)
        span = pl.ds(row, TILE)
        speed, eps, dlt, til, azi = (coef[owner, :, place, inner, :] for place in range(5))
        sin_t, cos_t = sin_cos(til)
        sin_a, cos_a = sin_cos_wide(azi)
        axis = (sin_t * cos_a, sin_t * sin_a, cos_t)
        turn = (cos_t * cos_a, cos_t * sin_a, -sin_t)
        quarter = tuple(0.25 * part for part in axis)
        stretch = 1.0 + 2.0 * eps
        root = jnp.sqrt(1.0 + 2.0 * dlt)
        for place, values in enumerate(axis + turn + (stretch, root, speed)):
            table[place, :, span, :] = values
        here_p, hess_p = hessian(pad_pq.at[0], row + PAD, first, last)
        here_q, hess_q = hessian(pad_pq.at[1], row + PAD, first, last)
        lean_p = times_axis(hess_p, axis, quarter)
        lean_q = times_axis(hess_q, axis, quarter)
        across = hess_p[0] + hess_p[1] + hess_p[2] - dot3(axis, lean_p)
        axial = dot3(axis, lean_q)
        drive_p = stretch * across + root * axial
        drive_q = root * across + axial
        pulse = at_source(row, wavelet[0, 0])
        here = pl.ds(pl.multiple_of(row + PAD, TILE), TILE)
        pad_next[0, 1:3, here, :] = 2.0 * here_p - olds[0, :, span, :] + speed * drive_p + pulse
        pad_next[1, 1:3, here, :] = 2.0 * here_q - olds[1, :, span, :] + speed * drive_q + pulse
        for place, values in enumerate(
            (
                across,
                axial,
                2.0 * dot3(turn, lean_p),
                2.0 * dot3(turn, lean_q),
                2.0 * (axis[0] * lean_p[1] - axis[1] * lean_p[0]),
                2.0 * (axis[0] * lean_q[1] - axis[1] * lean_q[0]),
            )
        ):
            terms[place, :, span, :] = values

    tiles = block // TILE

    def forward_block(place, carry):
        owner = step_of(place)

        @pl.when((place == 2) | (place == 3))
        def _():
            landed(coef.at[owner, place - 2], gather_recv.at[place - 2, place])

        @pl.when(place == 4)
        def _():
            pass_far(1)

        @pl.when((place == 4) | (place == 5))
        def _():
            landed(coef.at[owner, place - 4], gather_recv.at[place - 4, place])

        @pl.when(place >= 6)
        def _():
            for plane in range(2):
                landed(coef.at[owner, plane], gather_recv.at[plane, place])

        lax.fori_loop(0, tiles, lambda tile, c: (forward_tile(owner, tile), c)[1], 0)
        begin(next_halo(owner))
        return carry

    lax.fori_loop(0, blocks, forward_block, 0)

    arrived(halo_ab)

    def load_table(span):
        values = tuple(table[place, :, span, :] for place in range(9))
        return values[0:3], values[3:6], values[6], values[7], values[8]

    def adjoint_tile(owner, tile):
        row = pl.multiple_of(owner * block + tile * TILE, TILE)
        span = pl.ds(row, TILE)
        axis, _, stretch, root, speed = load_table(span)
        quarter = tuple(0.25 * part for part in axis)
        here_a, hess_a = hessian(pad_ab.at[0], row + PAD, first, last)
        here_b, hess_b = hessian(pad_ab.at[1], row + PAD, first, last)
        across = hess_a[0] + hess_a[1] + hess_a[2] - dot3(axis, times_axis(hess_a, axis, quarter))
        axial = dot3(axis, times_axis(hess_b, axis, quarter))
        step_a[0, :, span, :] = 2.0 * here_a - olds[2, :, span, :] + speed * (stretch * across + root * axial)
        step_a[1, :, span, :] = 2.0 * here_b - olds[3, :, span, :] + speed * (root * across + axial)

    def adjoint_block(place, carry):
        owner = step_of(place)
        lax.fori_loop(0, tiles, lambda tile, c: (adjoint_tile(owner, tile), c)[1], 0)
        return carry

    lax.fori_loop(6, blocks, adjoint_block, 0)

    def halo_in(owner, carry):
        arrived(next_halo(owner))
        return carry

    lax.fori_loop(0, blocks, halo_in, 0)

    def gradient_tile(owner, tile):
        inner = pl.ds(pl.multiple_of(tile * TILE, TILE), TILE)
        row = pl.multiple_of(owner * block + tile * TILE, TILE)
        span = pl.ds(row, TILE)
        axis, turn, stretch, root, speed = load_table(span)
        quarter = tuple(0.25 * part for part in axis)
        here_p, hess_p = hessian(pad_next.at[0], row + PAD, first, last)
        _, hess_q = hessian(pad_next.at[1], row + PAD, first, last)
        lean_p = times_axis(hess_p, axis, quarter)
        lean_q = times_axis(hess_q, axis, quarter)
        across1 = hess_p[0] + hess_p[1] + hess_p[2] - dot3(axis, lean_p)
        axial1 = dot3(axis, lean_q)
        here = pl.ds(pl.multiple_of(row + PAD, TILE), TILE)
        last_p = 2.0 * here_p - pad_pq[0, 1:3, here, :] + speed * (stretch * across1 + root * axial1)
        last_p = last_p + at_source(row, wavelet[0, 1])
        late_a, late_b = pad_ab[0, 1:3, here, :], pad_ab[1, 1:3, here, :]
        early_a = step_a[0, :, span, :] + (hits[0, :, span, :] * last_p - hits[1, :, span, :])
        early_b = step_a[1, :, span, :]
        across0, axial0, tilt_p0, tilt_q0, spin_p0, spin_q0 = (terms[place, :, span, :] for place in range(6))
        tilt_p1 = 2.0 * dot3(turn, lean_p)
        tilt_q1 = 2.0 * dot3(turn, lean_q)
        spin_p1 = 2.0 * (axis[0] * lean_p[1] - axis[1] * lean_p[0])
        spin_q1 = 2.0 * (axis[0] * lean_q[1] - axis[1] * lean_q[0])
        by_stretch = early_a * across0 + late_a * across1
        by_root = early_a * axial0 + early_b * across0 + late_a * axial1 + late_b * across1
        by_one = early_b * axial0 + late_b * axial1

        def turned(p0, q0, p1, q1):
            return speed * (
                root * (early_a * q0 - early_b * p0 + late_a * q1 - late_b * p1)
                - stretch * (early_a * p0 + late_a * p1)
                + (early_b * q0 + late_b * q1)
            )

        for place, values in enumerate(
            (
                stretch * by_stretch + root * by_root + by_one,
                2.0 * speed * by_stretch,
                speed * by_root / root,
                turned(tilt_p0, tilt_q0, tilt_p1, tilt_q1),
                turned(spin_p0, spin_q0, spin_p1, spin_q1),
            )
        ):
            grad[owner, :, place, inner, :] = values

    def far_part(side, where):
        return pltpu.make_async_remote_copy(
            src_ref=grad.at[other(2, where), side],
            dst_ref=far.at[side, where],
            send_sem=far_send.at[2 * side + where],
            recv_sem=far_recv.at[2 * side + where],
            device_id=((right, left)[side], domain),
            device_id_type=MESH,
        )

    def near_part(side, where, plane):
        return pltpu.make_async_remote_copy(
            src_ref=grad.at[other((1, 3)[side], where), plane],
            dst_ref=near.at[side, where, plane],
            send_sem=near_send.at[4 * side + 2 * where + plane],
            recv_sem=near_recv.at[4 * side + 2 * where + plane],
            device_id=((right, left)[side], domain),
            device_id_type=MESH,
        )

    def pass_sums(where):
        for side in range(2):
            owner = other((1, 3)[side], where)
            far_part(side, where).wait_recv()
            grad[owner, side] = grad[owner, side] + far[side, where]
            near_part(side, where, side).start()

    def gradient_block(turn_at, carry):
        place = jnp.where(
            turn_at < 2,
            7 - turn_at,
            jnp.where(turn_at < 4, turn_at + 2, jnp.where(turn_at < 6, turn_at - 2, 7 - turn_at)),
        )
        owner = step_of(place)

        @pl.when(turn_at == 2)
        def _():
            lax.fori_loop(0, 6, adjoint_block, 0)

        lax.fori_loop(0, tiles, lambda tile, c: (gradient_tile(owner, tile), c)[1], 0)
        for where in range(2):

            @pl.when(turn_at == 1 - where)
            def _():
                for side in range(2):
                    far_part(side, where).start()

            for side in range(2):

                @pl.when(turn_at == 4 - 2 * where + side)
                def _():
                    near_part(side, where, 1 - side).start()

            @pl.when(turn_at == 5 - 2 * where)
            def _():
                pass_sums(where)

        return carry

    lax.fori_loop(0, blocks, gradient_block, 0)

    swap = pltpu.make_async_remote_copy(
        src_ref=grad.at[mate],
        dst_ref=mates,
        send_sem=mate_send,
        recv_sem=mate_recv,
        device_id=(mate, domain),
        device_id_type=MESH,
    )
    for plane in range(2):
        for side in range(3):
            own_part(plane, side).wait_send()
        for side in range(2):
            mate_part(plane, side).wait_send()
            far_coef(plane, side).wait_send()
    sent(halo_pq)
    sent(halo_ab)

    def drained(owner, carry):
        sent(next_halo(owner))
        return carry

    lax.fori_loop(0, blocks, drained, 0)

    for side in range(2):
        for plane in range(2):
            near_part(side, 1, plane).wait_recv()
    grad[mate] = grad[mate] + (near[0, 1] + near[1, 1])
    swap.start()
    for side in range(2):
        for plane in range(2):
            near_part(side, 0, plane).wait_recv()
    total = grad[shot] + (near[0, 0] + near[1, 0])
    swap.wait_recv()
    total = total + mates[...]
    for plane in range(2):
        out[:, plane] = total[plane]

    for side in range(2):
        for where in range(2):
            far_part(side, where).wait_send()
            for plane in range(2):
                near_part(side, where, plane).wait_send()
    swap.wait_send()


def shards(velsq, epsilon, delta, tilt, azimuth, forward, adjoint, wavelet, source, receivers, observed):
    planes, block, lanes = velsq.shape
    rows = forward.shape[3]
    blocks = rows // block
    padded = pltpu.VMEM((2, planes + 2, rows + 2 * PAD, lanes), jnp.float32)
    anywhere = pl.BlockSpec(memory_space=pl.ANY)
    vmem = pl.BlockSpec(memory_space=pltpu.VMEM)

    def fields(*lead):
        return pltpu.VMEM(lead + (planes, rows, lanes), jnp.float32)

    def by_block(count):
        return pltpu.VMEM(count + (planes, 5, block, lanes), jnp.float32)

    sems = pltpu.SemaphoreType.DMA
    held = [
        pltpu.with_memory_space_constraint(values, pltpu.HBM)
        for values in (velsq, epsilon, delta, tilt, azimuth, forward, adjoint, wavelet, receivers, observed)
    ]
    return pl.pallas_call(
        kernel,
        out_shape=jax.ShapeDtypeStruct((5, planes, block, lanes), jnp.float32),
        in_specs=[anywhere] * 8 + [pl.BlockSpec(memory_space=pltpu.SMEM)] + [anywhere] * 2,
        out_specs=vmem,
        scratch_shapes=[pltpu.SMEM(wavelet.shape, jnp.float32)]
        + [pltpu.VMEM(receivers.shape, jnp.int32), pltpu.VMEM(observed.shape, jnp.float32)]
        + [by_block((blocks,))]
        + [padded] * 3
        + [fields(4), fields(9), fields(6), fields(2), fields(2), by_block((blocks,))]
        + [pltpu.VMEM((2, 2, 5, block, lanes), jnp.float32), by_block((2, 2)), by_block(())]
        + [
            sems((16,)),
            sems((14,)),
            sems((2, blocks)),
            sems((2, 2)),
            sems((2, 2)),
            sems((blocks, 2)),
            sems((blocks, 2)),
            sems((4,)),
            sems((4,)),
            sems((8,)),
            sems((8,)),
            sems(()),
            sems(()),
        ],
        compiler_params=pltpu.CompilerParams(
            collective_id=0, has_side_effects=True, vmem_limit_bytes=40 << 20
        ),
        name="gradient",
    )(*held[:8], source, *held[8:])


def solution(mesh):
    field = P("domain", "shot", None)
    state = P("shot", None, "domain", None, None)
    return jax.shard_map(
        shards,
        mesh=mesh,
        in_specs=(field,) * 5 + (state, state, P("shot", None), P("shot"), P("shot", None), P("shot", None, None)),
        out_specs=P(None, "domain", "shot", None),
        check_vma=False,
    )
```

```python
import functools

import jax
import jax.numpy as jnp
from jax import lax
from jax.experimental import pallas as pl
from jax.experimental.pallas import tpu as pltpu
from jax.sharding import PartitionSpec as P

MESH = pl.DeviceIdType.MESH
TILE = 8
PAD = 8


SIN = (1.0, -1 / 6, 1 / 120, -1 / 5040, 1 / 362880, -1 / 39916800, 1 / 6227020800)
COS = (1.0, -1 / 2, 1 / 24, -1 / 720, 1 / 40320, -1 / 3628800, 1 / 479001600, -1 / 87178291200)


def horner(square, series):
    total = jnp.float32(series[-1])
    for term in series[-2::-1]:
        total = total * square + jnp.float32(term)
    return total


def sin_cos(angle):
    square = angle * angle
    return angle * horner(square, SIN), horner(square, COS)


def sin_cos_wide(angle):
    half_sin, half_cos = sin_cos(0.5 * angle)
    return 2.0 * half_sin * half_cos, 1.0 - 2.0 * half_sin * half_sin


def hessian(pad_ref, row, first, last):
    here = pad_ref[:, pl.ds(row, TILE), :]
    above = pad_ref[:, pl.ds(row + 1, TILE), :]
    below = pad_ref[:, pl.ds(row - 1, TILE), :]

    def ahead(values):
        return jnp.where(last, 0.0, pltpu.roll(values, values.shape[-1] - 1, 2))

    def behind(values):
        return jnp.where(first, 0.0, pltpu.roll(values, 1, 2))

    center = here[1:3]
    twice = 2.0 * center
    along_x = here[2:4] - here[0:2]
    along_y = above[1:3] - below[1:3]
    xx = here[2:4] + here[0:2] - twice
    yy = above[1:3] + below[1:3] - twice
    zz = ahead(center) + behind(center) - twice
    xy = (above[2:4] - above[0:2]) - (below[2:4] - below[0:2])
    xz = ahead(along_x) - behind(along_x)
    yz = ahead(along_y) - behind(along_y)
    return center, (xx, yy, zz, xy, xz, yz)


def times_axis(parts, axis, quarter):
    xx, yy, zz, xy, xz, yz = parts
    return (
        xx * axis[0] + xy * quarter[1] + xz * quarter[2],
        xy * quarter[0] + yy * axis[1] + yz * quarter[2],
        xz * quarter[0] + yz * quarter[1] + zz * axis[2],
    )


def dot3(left, right):
    return left[0] * right[0] + left[1] * right[1] + left[2] * right[2]


def kernel(
    velsq,
    epsilon,
    delta,
    tilt,
    azimuth,
    forward,
    adjoint,
    wavelet_in,
    source,
    receivers_in,
    observed_in,
    out,
    wavelet,
    receivers,
    observed,
    coef,
    pad_pq,
    pad_ab,
    pad_next,
    olds,
    table,
    terms,
    step_a,
    hits,
    grad,
    far,
    near,
    mates,
    local_sem,
    gather_send,
    gather_recv,
    halo_send,
    halo_recv,
    next_send,
    next_recv,
    far_send,
    far_recv,
    near_send,
    near_recv,
    mate_send,
    mate_recv,
):
    shot = lax.axis_index("shot")
    domain = lax.axis_index("domain")
    slabs = lax.axis_size("domain")
    rows = pad_pq.shape[2] - 2 * PAD
    block = coef.shape[3]
    blocks = coef.shape[0]
    lanes = pad_pq.shape[3]
    has_low = domain > 0
    has_high = domain < slabs - 1

    def other(dx, dy):
        return lax.rem(shot // 2 + dx, 4) * 2 + lax.rem(lax.rem(shot, 2) + dy, 2)

    def step_of(place):
        dx = jnp.where(
            (place == 2) | (place == 4), 1, jnp.where((place == 3) | (place == 5), 3, jnp.where(place >= 6, 2, 0))
        )
        dy = jnp.where((place == 1) | (place == 4) | (place == 5) | (place == 7), 1, 0)
        return other(dx, dy)

    locals_ = []

    def local(src, dst):
        copy = pltpu.make_async_copy(src, dst, local_sem.at[len(locals_)])
        copy.start()
        locals_.append(copy)

    for place, field in enumerate((velsq, epsilon, delta, tilt, azimuth)):
        local(field, coef.at[shot, :, place])
    inside = pl.ds(PAD, rows)
    for pad, state in ((pad_pq, forward), (pad_ab, adjoint)):
        for place in range(2):
            local(state.at[0, 2 * place + 1], pad.at[place, pl.ds(1, 2), inside])
    for place, (state, member) in enumerate(((forward, 0), (forward, 2), (adjoint, 0), (adjoint, 2))):
        local(state.at[0, member], olds.at[place])

    for src, dst in ((wavelet_in, wavelet), (receivers_in, receivers), (observed_in, observed)):
        local(src, dst)

    barrier = pltpu.get_barrier_semaphore()
    mate, right, left = other(0, 1), other(1, 0), other(3, 0)
    for peer in (mate, right, left):
        pl.semaphore_signal(barrier, inc=1, device_id=(peer, domain), device_id_type=MESH)

    @pl.when(has_low)
    def _():
        pl.semaphore_signal(barrier, inc=1, device_id=(shot, domain - 1), device_id_type=MESH)

    @pl.when(has_high)
    def _():
        pl.semaphore_signal(barrier, inc=1, device_id=(shot, domain + 1), device_id_type=MESH)

    pads = (pad_pq, pad_ab, pad_next)
    for pad in pads:
        zero = jnp.zeros((2, 4, PAD, lanes), jnp.float32)
        pad[:, :, 0:PAD, :] = zero
        pad[:, :, PAD + rows : 2 * PAD + rows, :] = zero

    @pl.when(jnp.logical_not(has_low))
    def _():
        for pad in pads:
            pad[:, 0, PAD : PAD + rows, :] = jnp.zeros((2, rows, lanes), jnp.float32)

    @pl.when(jnp.logical_not(has_high))
    def _():
        for pad in pads:
            pad[:, 3, PAD : PAD + rows, :] = jnp.zeros((2, rows, lanes), jnp.float32)

    pl.semaphore_wait(barrier, 3 + has_low.astype(jnp.int32) + has_high.astype(jnp.int32))

    def halo(pad, span, send, recv, at):
        down = pltpu.make_async_remote_copy(
            src_ref=pad.at[:, 1, span],
            dst_ref=pad.at[:, 3, span],
            send_sem=send.at[at, 0],
            recv_sem=recv.at[at, 0],
            device_id=(shot, domain - 1),
            device_id_type=MESH,
        )
        up = pltpu.make_async_remote_copy(
            src_ref=pad.at[:, 2, span],
            dst_ref=pad.at[:, 0, span],
            send_sem=send.at[at, 1],
            recv_sem=recv.at[at, 1],
            device_id=(shot, domain + 1),
            device_id_type=MESH,
        )
        return down, up

    def begin(pair):
        pl.when(has_low)(pair[0].start)
        pl.when(has_high)(pair[1].start)

    def arrived(pair):
        pl.when(has_high)(pair[0].wait_recv)
        pl.when(has_low)(pair[1].wait_recv)

    def sent(pair):
        pl.when(has_low)(pair[0].wait_send)
        pl.when(has_high)(pair[1].wait_send)

    halo_pq = halo(pad_pq, inside, halo_send, halo_recv, 0)
    window = 2 * block

    def piece(step, offset, size, at):
        row = pl.multiple_of(lax.rem(shot // 2 + step, 4) * window + offset + PAD, TILE)
        return halo(pad_ab, pl.ds(row, size), halo_send, halo_recv, at)

    halo_ab = (piece(2, 0, window, 1), piece(3, 0, TILE, 2), piece(1, window - TILE, TILE, 3))
    halo_ab_late = (piece(1, 0, window - TILE, 4), piece(3, TILE, window - TILE, 5), piece(0, 0, window, 6))

    def push(part, peer, send_sem, recv_sem):
        return pltpu.make_async_remote_copy(
            src_ref=part,
            dst_ref=part,
            send_sem=send_sem,
            recv_sem=recv_sem,
            device_id=(peer, domain),
            device_id_type=MESH,
        )

    def landed(part, recv_sem):
        pltpu.make_async_copy(part, part, recv_sem).wait()

    def own_part(plane, side):
        return push(coef.at[shot, plane], (mate, right, left)[side], gather_send.at[3 * plane + side], gather_recv.at[plane, (1, 3, 2)[side]])

    def mate_part(plane, side):
        return push(coef.at[mate, plane], (right, left)[side], gather_send.at[6 + 2 * plane + side], gather_recv.at[plane, (5, 4)[side]])

    def far_coef(where, side):
        part = coef.at[other((3, 1)[side], where), side]
        return push(part, (right, left)[side], gather_send.at[10 + 2 * where + side], gather_recv.at[side, 6 + where])

    def pass_far(where):
        for side in range(2):
            owner = other((3, 1)[side], where)
            landed(coef.at[owner, side], gather_recv.at[side, (3, 2)[side] + 2 * where])
            far_coef(where, side).start()

    for copy in locals_[0:5]:
        copy.wait()
    for plane, side in ((0, 0), (0, 1), (1, 2), (1, 0), (1, 1), (0, 2)):
        own_part(plane, side).start()
    for copy in locals_[5:9]:
        copy.wait()
    begin(halo_pq)
    for copy in locals_[13:]:
        copy.wait()

    cells = receivers[...] - domain * (2 * rows * lanes)
    at_row = lax.shift_right_arithmetic(cells, 7)
    at_lane = cells & (lanes - 1)
    count = cells.shape[1]
    lane_of = lax.broadcasted_iota(jnp.int32, (lanes, count), 0)
    by_lane = jnp.where(lane_of == at_lane, 1.0, 0.0)
    recorded = by_lane * observed[0, 1:2, :]
    contract = (((1,), (1,)), ((), ()))
    for plane in range(2):
        row_of = lax.broadcasted_iota(jnp.int32, (rows, count), 0) + plane * rows
        by_row = jnp.where(row_of == at_row, 1.0, 0.0)
        hits[0, plane] = lax.dot_general(
            by_row, by_lane, contract, precision=lax.Precision.HIGHEST, preferred_element_type=jnp.float32
        )
        hits[1, plane] = lax.dot_general(
            by_row, recorded, contract, precision=lax.Precision.HIGHEST, preferred_element_type=jnp.float32
        )

    shape = (2, TILE, lanes)
    lane = lax.broadcasted_iota(jnp.int32, shape, 2)
    first = lane == 0
    last = lane == lanes - 1
    cell = lax.broadcasted_iota(jnp.int32, shape, 0) * (rows * lanes) + lax.broadcasted_iota(jnp.int32, shape, 1) * lanes + lane
    source_at = source[0] - domain * (2 * rows * lanes)

    def at_source(row, amount):
        return jnp.where(cell == source_at - row * lanes, amount, 0.0)

    for plane in range(2):
        landed(coef.at[mate, plane], gather_recv.at[plane, 1])
        mate_part(plane, plane).start()
        mate_part(plane, 1 - plane).start()
    pass_far(0)
    for pair in halo_ab:
        begin(pair)
    for copy in locals_[9:13]:
        copy.wait()
    arrived(halo_pq)

    def next_halo(owner):
        span = pl.ds(pl.multiple_of(owner * block + PAD, TILE), block)
        return halo(pad_next, span, next_send, next_recv, owner)

    def forward_tile(owner, tile):
        inner = pl.ds(pl.multiple_of(tile * TILE, TILE), TILE)
        row = pl.multiple_of(owner * block + tile * TILE, TILE)
        span = pl.ds(row, TILE)
        speed, eps, dlt, til, azi = (coef[owner, :, place, inner, :] for place in range(5))
        sin_t, cos_t = sin_cos(til)
        sin_a, cos_a = sin_cos_wide(azi)
        axis = (sin_t * cos_a, sin_t * sin_a, cos_t)
        turn = (cos_t * cos_a, cos_t * sin_a, -sin_t)
        quarter = tuple(0.25 * part for part in axis)
        stretch = 1.0 + 2.0 * eps
        root = jnp.sqrt(1.0 + 2.0 * dlt)
        for place, values in enumerate(axis + turn + (stretch, root, speed)):
            table[place, :, span, :] = values
        here_p, hess_p = hessian(pad_pq.at[0], row + PAD, first, last)
        here_q, hess_q = hessian(pad_pq.at[1], row + PAD, first, last)
        lean_p = times_axis(hess_p, axis, quarter)
        lean_q = times_axis(hess_q, axis, quarter)
        across = hess_p[0] + hess_p[1] + hess_p[2] - dot3(axis, lean_p)
        axial = dot3(axis, lean_q)
        drive_p = stretch * across + root * axial
        drive_q = root * across + axial
        pulse = at_source(row, wavelet[0, 0])
        here = pl.ds(pl.multiple_of(row + PAD, TILE), TILE)
        pad_next[0, 1:3, here, :] = 2.0 * here_p - olds[0, :, span, :] + speed * drive_p + pulse
        pad_next[1, 1:3, here, :] = 2.0 * here_q - olds[1, :, span, :] + speed * drive_q + pulse
        for place, values in enumerate(
            (
                across,
                axial,
                2.0 * dot3(turn, lean_p),
                2.0 * dot3(turn, lean_q),
                2.0 * (axis[0] * lean_p[1] - axis[1] * lean_p[0]),
                2.0 * (axis[0] * lean_q[1] - axis[1] * lean_q[0]),
            )
        ):
            terms[place, :, span, :] = values

    tiles = block // TILE

    def forward_block(place, carry):
        owner = step_of(place)

        @pl.when((place == 2) | (place == 3))
        def _():
            landed(coef.at[owner, place - 2], gather_recv.at[place - 2, place])

        @pl.when(place == 4)
        def _():
            pass_far(1)

        @pl.when((place == 4) | (place == 5))
        def _():
            landed(coef.at[owner, place - 4], gather_recv.at[place - 4, place])

        @pl.when(place >= 6)
        def _():
            for plane in range(2):
                landed(coef.at[owner, plane], gather_recv.at[plane, place])

        lax.fori_loop(0, tiles, lambda tile, c: (forward_tile(owner, tile), c)[1], 0, unroll=4)

        @pl.when(place >= 2)
        def _():
            begin(next_halo(owner))

        return carry

    lax.fori_loop(0, blocks, forward_block, 0)

    for place in range(2):
        begin(next_halo(step_of(place)))
    for pair in halo_ab_late:
        begin(pair)
    for pair in halo_ab:
        arrived(pair)

    def load_table(span):
        values = tuple(table[place, :, span, :] for place in range(9))
        return values[0:3], values[3:6], values[6], values[7], values[8]

    def adjoint_tile(owner, tile):
        row = pl.multiple_of(owner * block + tile * TILE, TILE)
        span = pl.ds(row, TILE)
        axis, _, stretch, root, speed = load_table(span)
        quarter = tuple(0.25 * part for part in axis)
        here_a, hess_a = hessian(pad_ab.at[0], row + PAD, first, last)
        here_b, hess_b = hessian(pad_ab.at[1], row + PAD, first, last)
        across = hess_a[0] + hess_a[1] + hess_a[2] - dot3(axis, times_axis(hess_a, axis, quarter))
        axial = dot3(axis, times_axis(hess_b, axis, quarter))
        step_a[0, :, span, :] = 2.0 * here_a - olds[2, :, span, :] + speed * (stretch * across + root * axial)
        step_a[1, :, span, :] = 2.0 * here_b - olds[3, :, span, :] + speed * (root * across + axial)

    def adjoint_block(place, carry):
        owner = step_of(place)
        lax.fori_loop(0, tiles, lambda tile, c: (adjoint_tile(owner, tile), c)[1], 0, unroll=4)
        return carry

    lax.fori_loop(6, blocks, adjoint_block, 0)

    def halo_in(steps):
        for step, y in steps:
            arrived(next_halo(lax.rem(shot // 2 + step, 4) * 2 + y))

    halo_in(((2, 0), (2, 1), (1, 1), (3, 0)))

    def gradient_tile(owner, tile):
        inner = pl.ds(pl.multiple_of(tile * TILE, TILE), TILE)
        row = pl.multiple_of(owner * block + tile * TILE, TILE)
        span = pl.ds(row, TILE)
        axis, turn, stretch, root, speed = load_table(span)
        quarter = tuple(0.25 * part for part in axis)
        here_p, hess_p = hessian(pad_next.at[0], row + PAD, first, last)
        _, hess_q = hessian(pad_next.at[1], row + PAD, first, last)
        lean_p = times_axis(hess_p, axis, quarter)
        lean_q = times_axis(hess_q, axis, quarter)
        across1 = hess_p[0] + hess_p[1] + hess_p[2] - dot3(axis, lean_p)
        axial1 = dot3(axis, lean_q)
        here = pl.ds(pl.multiple_of(row + PAD, TILE), TILE)
        last_p = 2.0 * here_p - pad_pq[0, 1:3, here, :] + speed * (stretch * across1 + root * axial1)
        last_p = last_p + at_source(row, wavelet[0, 1])
        late_a, late_b = pad_ab[0, 1:3, here, :], pad_ab[1, 1:3, here, :]
        early_a = step_a[0, :, span, :] + (hits[0, :, span, :] * last_p - hits[1, :, span, :])
        early_b = step_a[1, :, span, :]
        across0, axial0, tilt_p0, tilt_q0, spin_p0, spin_q0 = (terms[place, :, span, :] for place in range(6))
        tilt_p1 = 2.0 * dot3(turn, lean_p)
        tilt_q1 = 2.0 * dot3(turn, lean_q)
        spin_p1 = 2.0 * (axis[0] * lean_p[1] - axis[1] * lean_p[0])
        spin_q1 = 2.0 * (axis[0] * lean_q[1] - axis[1] * lean_q[0])
        by_stretch = early_a * across0 + late_a * across1
        by_root = early_a * axial0 + early_b * across0 + late_a * axial1 + late_b * across1
        by_one = early_b * axial0 + late_b * axial1

        def turned(p0, q0, p1, q1):
            return speed * (
                root * (early_a * q0 - early_b * p0 + late_a * q1 - late_b * p1)
                - stretch * (early_a * p0 + late_a * p1)
                + (early_b * q0 + late_b * q1)
            )

        for place, values in enumerate(
            (
                stretch * by_stretch + root * by_root + by_one,
                2.0 * speed * by_stretch,
                speed * by_root / root,
                turned(tilt_p0, tilt_q0, tilt_p1, tilt_q1),
                turned(spin_p0, spin_q0, spin_p1, spin_q1),
            )
        ):
            grad[owner, :, place, inner, :] = values

    def far_part(side, where):
        return pltpu.make_async_remote_copy(
            src_ref=grad.at[other(2, where), side],
            dst_ref=far.at[side, where],
            send_sem=far_send.at[2 * side + where],
            recv_sem=far_recv.at[2 * side + where],
            device_id=((right, left)[side], domain),
            device_id_type=MESH,
        )

    def near_part(side, where, plane):
        return pltpu.make_async_remote_copy(
            src_ref=grad.at[other((1, 3)[side], where), plane],
            dst_ref=near.at[side, where, plane],
            send_sem=near_send.at[4 * side + 2 * where + plane],
            recv_sem=near_recv.at[4 * side + 2 * where + plane],
            device_id=((right, left)[side], domain),
            device_id_type=MESH,
        )

    def pass_sums(where):
        for side in range(2):
            owner = other((1, 3)[side], where)
            far_part(side, where).wait_recv()
            grad[owner, side] = grad[owner, side] + far[side, where]
            near_part(side, where, side).start()

    def gradient_block(turn_at, carry):
        place = jnp.where(
            turn_at < 2,
            7 - turn_at,
            jnp.where(turn_at < 4, turn_at + 2, jnp.where(turn_at < 6, turn_at - 2, 7 - turn_at)),
        )
        owner = step_of(place)

        @pl.when(turn_at == 2)
        def _():
            halo_in(((1, 0), (3, 1), (0, 0), (0, 1)))
            for pair in halo_ab_late:
                arrived(pair)

        @pl.when(turn_at >= 2)
        def _():
            adjoint_block(place, 0)

        lax.fori_loop(0, tiles, lambda tile, c: (gradient_tile(owner, tile), c)[1], 0, unroll=4)
        for where in range(2):

            @pl.when(turn_at == 1 - where)
            def _():
                for side in range(2):
                    far_part(side, where).start()

            for side in range(2):

                @pl.when(turn_at == 4 - 2 * where + side)
                def _():
                    near_part(side, where, 1 - side).start()

            @pl.when(turn_at == 5 - 2 * where)
            def _():
                pass_sums(where)

        return carry

    lax.fori_loop(0, blocks, gradient_block, 0)

    swap = pltpu.make_async_remote_copy(
        src_ref=grad.at[mate],
        dst_ref=mates,
        send_sem=mate_send,
        recv_sem=mate_recv,
        device_id=(mate, domain),
        device_id_type=MESH,
    )
    for plane in range(2):
        for side in range(3):
            own_part(plane, side).wait_send()
        for side in range(2):
            mate_part(plane, side).wait_send()
            far_coef(plane, side).wait_send()
    sent(halo_pq)
    for pair in halo_ab + halo_ab_late:
        sent(pair)

    def drained(owner, carry):
        sent(next_halo(owner))
        return carry

    lax.fori_loop(0, blocks, drained, 0)

    for side in range(2):
        for plane in range(2):
            near_part(side, 1, plane).wait_recv()
    grad[mate] = grad[mate] + (near[0, 1] + near[1, 1])
    swap.start()
    for side in range(2):
        for plane in range(2):
            near_part(side, 0, plane).wait_recv()
    total = grad[shot] + (near[0, 0] + near[1, 0])
    swap.wait_recv()
    total = total + mates[...]
    for plane in range(2):
        out[:, plane] = total[plane]

    for side in range(2):
        for where in range(2):
            far_part(side, where).wait_send()
            for plane in range(2):
                near_part(side, where, plane).wait_send()
    swap.wait_send()


def shards(velsq, epsilon, delta, tilt, azimuth, forward, adjoint, wavelet, source, receivers, observed):
    planes, block, lanes = velsq.shape
    rows = forward.shape[3]
    blocks = rows // block
    padded = pltpu.VMEM((2, planes + 2, rows + 2 * PAD, lanes), jnp.float32)
    anywhere = pl.BlockSpec(memory_space=pl.ANY)
    vmem = pl.BlockSpec(memory_space=pltpu.VMEM)

    def fields(*lead):
        return pltpu.VMEM(lead + (planes, rows, lanes), jnp.float32)

    def by_block(count):
        return pltpu.VMEM(count + (planes, 5, block, lanes), jnp.float32)

    sems = pltpu.SemaphoreType.DMA
    held = [
        pltpu.with_memory_space_constraint(values, pltpu.HBM)
        for values in (velsq, epsilon, delta, tilt, azimuth, forward, adjoint, wavelet, receivers, observed)
    ]
    return pl.pallas_call(
        kernel,
        out_shape=jax.ShapeDtypeStruct((5, planes, block, lanes), jnp.float32),
        in_specs=[anywhere] * 8 + [pl.BlockSpec(memory_space=pltpu.SMEM)] + [anywhere] * 2,
        out_specs=vmem,
        scratch_shapes=[pltpu.SMEM(wavelet.shape, jnp.float32)]
        + [pltpu.VMEM(receivers.shape, jnp.int32), pltpu.VMEM(observed.shape, jnp.float32)]
        + [by_block((blocks,))]
        + [padded] * 3
        + [fields(4), fields(9), fields(6), fields(2), fields(2), by_block((blocks,))]
        + [pltpu.VMEM((2, 2, 5, block, lanes), jnp.float32), by_block((2, 2)), by_block(())]
        + [
            sems((16,)),
            sems((14,)),
            sems((2, blocks)),
            sems((7, 2)),
            sems((7, 2)),
            sems((blocks, 2)),
            sems((blocks, 2)),
            sems((4,)),
            sems((4,)),
            sems((8,)),
            sems((8,)),
            sems(()),
            sems(()),
        ],
        compiler_params=pltpu.CompilerParams(
            collective_id=0, has_side_effects=True, vmem_limit_bytes=40 << 20
        ),
        name="gradient",
    )(*held[:8], source, *held[8:])


def solution(mesh):
    field = P("domain", "shot", None)
    state = P("shot", None, "domain", None, None)
    return jax.shard_map(
        shards,
        mesh=mesh,
        in_specs=(field,) * 5 + (state, state, P("shot", None), P("shot"), P("shot", None), P("shot", None, None)),
        out_specs=P(None, "domain", "shot", None),
        check_vma=False,
    )
```

```python
import functools

import jax
import jax.numpy as jnp
from jax import lax
from jax.experimental import pallas as pl
from jax.experimental.pallas import tpu as pltpu
from jax.sharding import PartitionSpec as P

MESH = pl.DeviceIdType.MESH
TILE = 8
PAD = 8


SIN = (1.0, -1 / 6, 1 / 120, -1 / 5040, 1 / 362880, -1 / 39916800, 1 / 6227020800)
COS = (1.0, -1 / 2, 1 / 24, -1 / 720, 1 / 40320, -1 / 3628800, 1 / 479001600, -1 / 87178291200)


def horner(square, series):
    total = jnp.float32(series[-1])
    for term in series[-2::-1]:
        total = total * square + jnp.float32(term)
    return total


def sin_cos(angle):
    square = angle * angle
    return angle * horner(square, SIN), horner(square, COS)


def sin_cos_wide(angle):
    half_sin, half_cos = sin_cos(0.5 * angle)
    return 2.0 * half_sin * half_cos, 1.0 - 2.0 * half_sin * half_sin


def hessian(pad_ref, row, first, last):
    here = pad_ref[:, pl.ds(row, TILE), :]
    above = pad_ref[:, pl.ds(row + 1, TILE), :]
    below = pad_ref[:, pl.ds(row - 1, TILE), :]

    def ahead(values):
        return jnp.where(last, 0.0, pltpu.roll(values, values.shape[-1] - 1, 2))

    def behind(values):
        return jnp.where(first, 0.0, pltpu.roll(values, 1, 2))

    center = here[1:3]
    twice = 2.0 * center
    along_x = here[2:4] - here[0:2]
    along_y = above[1:3] - below[1:3]
    xx = here[2:4] + here[0:2] - twice
    yy = above[1:3] + below[1:3] - twice
    zz = ahead(center) + behind(center) - twice
    xy = (above[2:4] - above[0:2]) - (below[2:4] - below[0:2])
    xz = ahead(along_x) - behind(along_x)
    yz = ahead(along_y) - behind(along_y)
    return center, (xx, yy, zz, xy, xz, yz)


def times_axis(parts, axis, quarter):
    xx, yy, zz, xy, xz, yz = parts
    return (
        xx * axis[0] + xy * quarter[1] + xz * quarter[2],
        xy * quarter[0] + yy * axis[1] + yz * quarter[2],
        xz * quarter[0] + yz * quarter[1] + zz * axis[2],
    )


def dot3(left, right):
    return left[0] * right[0] + left[1] * right[1] + left[2] * right[2]


def kernel(
    velsq,
    epsilon,
    delta,
    tilt,
    azimuth,
    forward,
    adjoint,
    wavelet_in,
    source,
    receivers_in,
    observed_in,
    out,
    wavelet,
    receivers,
    observed,
    coef,
    pad_pq,
    pad_ab,
    pad_next,
    olds,
    table,
    terms,
    step_a,
    hits,
    grad,
    far,
    near,
    mates,
    local_sem,
    gather_send,
    gather_recv,
    halo_send,
    halo_recv,
    next_send,
    next_recv,
    far_send,
    far_recv,
    near_send,
    near_recv,
    mate_send,
    mate_recv,
):
    shot = lax.axis_index("shot")
    domain = lax.axis_index("domain")
    slabs = lax.axis_size("domain")
    rows = pad_pq.shape[2] - 2 * PAD
    block = coef.shape[3]
    blocks = coef.shape[0]
    lanes = pad_pq.shape[3]
    has_low = domain > 0
    has_high = domain < slabs - 1

    def other(dx, dy):
        return lax.rem(shot // 2 + dx, 4) * 2 + lax.rem(lax.rem(shot, 2) + dy, 2)

    def step_of(place):
        dx = jnp.where(
            (place == 2) | (place == 4), 1, jnp.where((place == 3) | (place == 5), 3, jnp.where(place >= 6, 2, 0))
        )
        dy = jnp.where((place == 1) | (place == 4) | (place == 5) | (place == 7), 1, 0)
        return other(dx, dy)

    locals_ = []

    def local(src, dst):
        copy = pltpu.make_async_copy(src, dst, local_sem.at[len(locals_)])
        copy.start()
        locals_.append(copy)

    for place, field in enumerate((velsq, epsilon, delta, tilt, azimuth)):
        local(field, coef.at[shot, :, place])
    inside = pl.ds(PAD, rows)
    for pad, state in ((pad_pq, forward), (pad_ab, adjoint)):
        for place in range(2):
            local(state.at[0, 2 * place + 1], pad.at[place, pl.ds(1, 2), inside])
    for place, (state, member) in enumerate(((forward, 0), (forward, 2), (adjoint, 0), (adjoint, 2))):
        local(state.at[0, member], olds.at[place])

    for src, dst in ((wavelet_in, wavelet), (receivers_in, receivers), (observed_in, observed)):
        local(src, dst)

    barrier = pltpu.get_barrier_semaphore()
    mate, right, left = other(0, 1), other(1, 0), other(3, 0)
    for peer in (mate, right, left):
        pl.semaphore_signal(barrier, inc=1, device_id=(peer, domain), device_id_type=MESH)

    @pl.when(has_low)
    def _():
        pl.semaphore_signal(barrier, inc=1, device_id=(shot, domain - 1), device_id_type=MESH)

    @pl.when(has_high)
    def _():
        pl.semaphore_signal(barrier, inc=1, device_id=(shot, domain + 1), device_id_type=MESH)

    pads = (pad_pq, pad_ab, pad_next)
    for pad in pads:
        zero = jnp.zeros((2, 4, PAD, lanes), jnp.float32)
        pad[:, :, 0:PAD, :] = zero
        pad[:, :, PAD + rows : 2 * PAD + rows, :] = zero

    @pl.when(jnp.logical_not(has_low))
    def _():
        for pad in pads:
            pad[:, 0, PAD : PAD + rows, :] = jnp.zeros((2, rows, lanes), jnp.float32)

    @pl.when(jnp.logical_not(has_high))
    def _():
        for pad in pads:
            pad[:, 3, PAD : PAD + rows, :] = jnp.zeros((2, rows, lanes), jnp.float32)

    pl.semaphore_wait(barrier, 3 + has_low.astype(jnp.int32) + has_high.astype(jnp.int32))

    def halo(pad, span, send, recv, at):
        down = pltpu.make_async_remote_copy(
            src_ref=pad.at[:, 1, span],
            dst_ref=pad.at[:, 3, span],
            send_sem=send.at[at, 0],
            recv_sem=recv.at[at, 0],
            device_id=(shot, domain - 1),
            device_id_type=MESH,
        )
        up = pltpu.make_async_remote_copy(
            src_ref=pad.at[:, 2, span],
            dst_ref=pad.at[:, 0, span],
            send_sem=send.at[at, 1],
            recv_sem=recv.at[at, 1],
            device_id=(shot, domain + 1),
            device_id_type=MESH,
        )
        return down, up

    def begin(pair):
        pl.when(has_low)(pair[0].start)
        pl.when(has_high)(pair[1].start)

    def arrived(pair):
        pl.when(has_high)(pair[0].wait_recv)
        pl.when(has_low)(pair[1].wait_recv)

    def sent(pair):
        pl.when(has_low)(pair[0].wait_send)
        pl.when(has_high)(pair[1].wait_send)

    halo_pq = halo(pad_pq, inside, halo_send, halo_recv, 0)
    window = 2 * block

    def piece(step, offset, size, at):
        row = pl.multiple_of(lax.rem(shot // 2 + step, 4) * window + offset + PAD, TILE)
        return halo(pad_ab, pl.ds(row, size), halo_send, halo_recv, at)

    halo_ab = (piece(2, 0, window, 1), piece(3, 0, TILE, 2), piece(1, window - TILE, TILE, 3))
    halo_ab_late = (piece(1, 0, window - TILE, 4), piece(3, TILE, window - TILE, 5), piece(0, 0, window, 6))

    def push(part, peer, send_sem, recv_sem):
        return pltpu.make_async_remote_copy(
            src_ref=part,
            dst_ref=part,
            send_sem=send_sem,
            recv_sem=recv_sem,
            device_id=(peer, domain),
            device_id_type=MESH,
        )

    def landed(part, recv_sem):
        pltpu.make_async_copy(part, part, recv_sem).wait()

    def own_part(plane, side):
        return push(coef.at[shot, plane], (mate, right, left)[side], gather_send.at[3 * plane + side], gather_recv.at[plane, (1, 3, 2)[side]])

    def mate_part(plane, side):
        return push(coef.at[mate, plane], (right, left)[side], gather_send.at[6 + 2 * plane + side], gather_recv.at[plane, (5, 4)[side]])

    def far_coef(where, side):
        part = coef.at[other((3, 1)[side], where), side]
        return push(part, (right, left)[side], gather_send.at[10 + 2 * where + side], gather_recv.at[side, 6 + where])

    def pass_far(where):
        for side in range(2):
            owner = other((3, 1)[side], where)
            landed(coef.at[owner, side], gather_recv.at[side, (3, 2)[side] + 2 * where])
            far_coef(where, side).start()

    for copy in locals_[0:5]:
        copy.wait()
    for plane, side in ((0, 0), (0, 1), (1, 2), (1, 0), (1, 1), (0, 2)):
        own_part(plane, side).start()
    for copy in locals_[5:9]:
        copy.wait()
    begin(halo_pq)
    for copy in locals_[13:]:
        copy.wait()

    cells = receivers[...] - domain * (2 * rows * lanes)
    at_row = lax.shift_right_arithmetic(cells, 7)
    at_lane = cells & (lanes - 1)
    count = cells.shape[1]
    lane_of = lax.broadcasted_iota(jnp.int32, (lanes, count), 0)
    by_lane = jnp.where(lane_of == at_lane, 1.0, 0.0)
    recorded = by_lane * observed[0, 1:2, :]
    contract = (((1,), (1,)), ((), ()))
    for plane in range(2):
        row_of = lax.broadcasted_iota(jnp.int32, (rows, count), 0) + plane * rows
        by_row = jnp.where(row_of == at_row, 1.0, 0.0)
        hits[0, plane] = lax.dot_general(
            by_row, by_lane, contract, precision=lax.Precision.HIGHEST, preferred_element_type=jnp.float32
        )
        hits[1, plane] = lax.dot_general(
            by_row, recorded, contract, precision=lax.Precision.HIGHEST, preferred_element_type=jnp.float32
        )

    shape = (2, TILE, lanes)
    lane = lax.broadcasted_iota(jnp.int32, shape, 2)
    first = lane == 0
    last = lane == lanes - 1
    cell = lax.broadcasted_iota(jnp.int32, shape, 0) * (rows * lanes) + lax.broadcasted_iota(jnp.int32, shape, 1) * lanes + lane
    source_at = source[0] - domain * (2 * rows * lanes)

    def at_source(row, amount):
        return jnp.where(cell == source_at - row * lanes, amount, 0.0)

    for plane in range(2):
        landed(coef.at[mate, plane], gather_recv.at[plane, 1])
        mate_part(plane, plane).start()
        mate_part(plane, 1 - plane).start()
    pass_far(0)
    for pair in halo_ab:
        begin(pair)
    for copy in locals_[9:13]:
        copy.wait()
    arrived(halo_pq)

    def next_halo(owner):
        span = pl.ds(pl.multiple_of(owner * block + PAD, TILE), block)
        return halo(pad_next, span, next_send, next_recv, owner)

    def forward_tile(owner, tile):
        inner = pl.ds(pl.multiple_of(tile * TILE, TILE), TILE)
        row = pl.multiple_of(owner * block + tile * TILE, TILE)
        span = pl.ds(row, TILE)
        speed, eps, dlt, til, azi = (coef[owner, :, place, inner, :] for place in range(5))
        sin_t, cos_t = sin_cos(til)
        sin_a, cos_a = sin_cos_wide(azi)
        axis = (sin_t * cos_a, sin_t * sin_a, cos_t)
        turn = (cos_t * cos_a, cos_t * sin_a, -sin_t)
        quarter = tuple(0.25 * part for part in axis)
        stretch = 1.0 + 2.0 * eps
        root = jnp.sqrt(1.0 + 2.0 * dlt)
        for place, values in enumerate(axis + turn + (stretch, root, speed)):
            table[place, :, span, :] = values
        here_p, hess_p = hessian(pad_pq.at[0], row + PAD, first, last)
        here_q, hess_q = hessian(pad_pq.at[1], row + PAD, first, last)
        lean_p = times_axis(hess_p, axis, quarter)
        lean_q = times_axis(hess_q, axis, quarter)
        across = hess_p[0] + hess_p[1] + hess_p[2] - dot3(axis, lean_p)
        axial = dot3(axis, lean_q)
        drive_p = stretch * across + root * axial
        drive_q = root * across + axial
        pulse = at_source(row, wavelet[0, 0])
        here = pl.ds(pl.multiple_of(row + PAD, TILE), TILE)
        pad_next[0, 1:3, here, :] = 2.0 * here_p - olds[0, :, span, :] + speed * drive_p + pulse
        pad_next[1, 1:3, here, :] = 2.0 * here_q - olds[1, :, span, :] + speed * drive_q + pulse
        for place, values in enumerate(
            (
                across,
                axial,
                2.0 * dot3(turn, lean_p),
                2.0 * dot3(turn, lean_q),
                2.0 * (axis[0] * lean_p[1] - axis[1] * lean_p[0]),
                2.0 * (axis[0] * lean_q[1] - axis[1] * lean_q[0]),
            )
        ):
            terms[place, :, span, :] = values

    tiles = block // TILE

    def forward_block(turn_at, carry):
        place = jnp.where(turn_at < 2, turn_at + 2, jnp.where(turn_at < 4, turn_at - 2, turn_at))
        owner = step_of(place)

        @pl.when((place == 2) | (place == 3))
        def _():
            landed(coef.at[owner, place - 2], gather_recv.at[place - 2, place])

        @pl.when(place == 4)
        def _():
            pass_far(1)

        @pl.when((place == 4) | (place == 5))
        def _():
            landed(coef.at[owner, place - 4], gather_recv.at[place - 4, place])

        @pl.when(place >= 6)
        def _():
            for plane in range(2):
                landed(coef.at[owner, plane], gather_recv.at[plane, place])

        lax.fori_loop(0, tiles, lambda tile, c: (forward_tile(owner, tile), c)[1], 0, unroll=4)

        @pl.when(place >= 2)
        def _():
            begin(next_halo(owner))

        return carry

    lax.fori_loop(0, blocks, forward_block, 0)

    for place in range(2):
        begin(next_halo(step_of(place)))
    for pair in halo_ab_late:
        begin(pair)
    for pair in halo_ab:
        arrived(pair)

    def load_table(span):
        values = tuple(table[place, :, span, :] for place in range(9))
        return values[0:3], values[3:6], values[6], values[7], values[8]

    def adjoint_tile(owner, tile):
        row = pl.multiple_of(owner * block + tile * TILE, TILE)
        span = pl.ds(row, TILE)
        axis, _, stretch, root, speed = load_table(span)
        quarter = tuple(0.25 * part for part in axis)
        here_a, hess_a = hessian(pad_ab.at[0], row + PAD, first, last)
        here_b, hess_b = hessian(pad_ab.at[1], row + PAD, first, last)
        across = hess_a[0] + hess_a[1] + hess_a[2] - dot3(axis, times_axis(hess_a, axis, quarter))
        axial = dot3(axis, times_axis(hess_b, axis, quarter))
        step_a[0, :, span, :] = 2.0 * here_a - olds[2, :, span, :] + speed * (stretch * across + root * axial)
        step_a[1, :, span, :] = 2.0 * here_b - olds[3, :, span, :] + speed * (root * across + axial)

    def adjoint_block(place, carry):
        owner = step_of(place)
        lax.fori_loop(0, tiles, lambda tile, c: (adjoint_tile(owner, tile), c)[1], 0, unroll=4)
        return carry

    lax.fori_loop(6, blocks, adjoint_block, 0)

    def halo_in(steps):
        for step, y in steps:
            arrived(next_halo(lax.rem(shot // 2 + step, 4) * 2 + y))

    halo_in(((2, 0), (2, 1), (1, 1), (3, 0)))

    def gradient_tile(owner, tile):
        inner = pl.ds(pl.multiple_of(tile * TILE, TILE), TILE)
        row = pl.multiple_of(owner * block + tile * TILE, TILE)
        span = pl.ds(row, TILE)
        axis, turn, stretch, root, speed = load_table(span)
        quarter = tuple(0.25 * part for part in axis)
        here_p, hess_p = hessian(pad_next.at[0], row + PAD, first, last)
        _, hess_q = hessian(pad_next.at[1], row + PAD, first, last)
        lean_p = times_axis(hess_p, axis, quarter)
        lean_q = times_axis(hess_q, axis, quarter)
        across1 = hess_p[0] + hess_p[1] + hess_p[2] - dot3(axis, lean_p)
        axial1 = dot3(axis, lean_q)
        here = pl.ds(pl.multiple_of(row + PAD, TILE), TILE)
        last_p = 2.0 * here_p - pad_pq[0, 1:3, here, :] + speed * (stretch * across1 + root * axial1)
        last_p = last_p + at_source(row, wavelet[0, 1])
        late_a, late_b = pad_ab[0, 1:3, here, :], pad_ab[1, 1:3, here, :]
        early_a = step_a[0, :, span, :] + (hits[0, :, span, :] * last_p - hits[1, :, span, :])
        early_b = step_a[1, :, span, :]
        across0, axial0, tilt_p0, tilt_q0, spin_p0, spin_q0 = (terms[place, :, span, :] for place in range(6))
        tilt_p1 = 2.0 * dot3(turn, lean_p)
        tilt_q1 = 2.0 * dot3(turn, lean_q)
        spin_p1 = 2.0 * (axis[0] * lean_p[1] - axis[1] * lean_p[0])
        spin_q1 = 2.0 * (axis[0] * lean_q[1] - axis[1] * lean_q[0])
        by_stretch = early_a * across0 + late_a * across1
        by_root = early_a * axial0 + early_b * across0 + late_a * axial1 + late_b * across1
        by_one = early_b * axial0 + late_b * axial1

        def turned(p0, q0, p1, q1):
            return speed * (
                root * (early_a * q0 - early_b * p0 + late_a * q1 - late_b * p1)
                - stretch * (early_a * p0 + late_a * p1)
                + (early_b * q0 + late_b * q1)
            )

        for place, values in enumerate(
            (
                stretch * by_stretch + root * by_root + by_one,
                2.0 * speed * by_stretch,
                speed * by_root / root,
                turned(tilt_p0, tilt_q0, tilt_p1, tilt_q1),
                turned(spin_p0, spin_q0, spin_p1, spin_q1),
            )
        ):
            grad[owner, :, place, inner, :] = values

    def far_part(side, where):
        return pltpu.make_async_remote_copy(
            src_ref=grad.at[other(2, where), side],
            dst_ref=far.at[side, where],
            send_sem=far_send.at[2 * side + where],
            recv_sem=far_recv.at[2 * side + where],
            device_id=((right, left)[side], domain),
            device_id_type=MESH,
        )

    def near_part(side, where, plane):
        return pltpu.make_async_remote_copy(
            src_ref=grad.at[other((1, 3)[side], where), plane],
            dst_ref=near.at[side, where, plane],
            send_sem=near_send.at[4 * side + 2 * where + plane],
            recv_sem=near_recv.at[4 * side + 2 * where + plane],
            device_id=((right, left)[side], domain),
            device_id_type=MESH,
        )

    def pass_sums(where):
        for side in range(2):
            owner = other((1, 3)[side], where)
            far_part(side, where).wait_recv()
            grad[owner, side] = grad[owner, side] + far[side, where]
            near_part(side, where, side).start()

    def gradient_block(turn_at, carry):
        place = jnp.where(
            turn_at < 2,
            7 - turn_at,
            jnp.where(turn_at < 4, turn_at + 2, jnp.where(turn_at < 6, turn_at - 2, 7 - turn_at)),
        )
        owner = step_of(place)

        @pl.when(turn_at == 2)
        def _():
            halo_in(((1, 0), (3, 1), (0, 0), (0, 1)))
            for pair in halo_ab_late:
                arrived(pair)

        @pl.when(turn_at >= 2)
        def _():
            adjoint_block(place, 0)

        lax.fori_loop(0, tiles, lambda tile, c: (gradient_tile(owner, tile), c)[1], 0, unroll=4)
        for where in range(2):

            @pl.when(turn_at == 1 - where)
            def _():
                for side in range(2):
                    far_part(side, where).start()

            for side in range(2):

                @pl.when(turn_at == 4 - 2 * where + side)
                def _():
                    near_part(side, where, 1 - side).start()

            @pl.when(turn_at == 5 - 2 * where)
            def _():
                pass_sums(where)

        return carry

    lax.fori_loop(0, blocks, gradient_block, 0)

    swap = pltpu.make_async_remote_copy(
        src_ref=grad.at[mate],
        dst_ref=mates,
        send_sem=mate_send,
        recv_sem=mate_recv,
        device_id=(mate, domain),
        device_id_type=MESH,
    )
    for plane in range(2):
        for side in range(3):
            own_part(plane, side).wait_send()
        for side in range(2):
            mate_part(plane, side).wait_send()
            far_coef(plane, side).wait_send()
    sent(halo_pq)
    for pair in halo_ab + halo_ab_late:
        sent(pair)

    def drained(owner, carry):
        sent(next_halo(owner))
        return carry

    lax.fori_loop(0, blocks, drained, 0)

    for side in range(2):
        for plane in range(2):
            near_part(side, 1, plane).wait_recv()
    grad[mate] = grad[mate] + (near[0, 1] + near[1, 1])
    swap.start()
    for side in range(2):
        for plane in range(2):
            near_part(side, 0, plane).wait_recv()
    total = grad[shot] + (near[0, 0] + near[1, 0])
    swap.wait_recv()
    total = total + mates[...]
    for plane in range(2):
        out[:, plane] = total[plane]

    for side in range(2):
        for where in range(2):
            far_part(side, where).wait_send()
            for plane in range(2):
                near_part(side, where, plane).wait_send()
    swap.wait_send()


def shards(velsq, epsilon, delta, tilt, azimuth, forward, adjoint, wavelet, source, receivers, observed):
    planes, block, lanes = velsq.shape
    rows = forward.shape[3]
    blocks = rows // block
    padded = pltpu.VMEM((2, planes + 2, rows + 2 * PAD, lanes), jnp.float32)
    anywhere = pl.BlockSpec(memory_space=pl.ANY)
    vmem = pl.BlockSpec(memory_space=pltpu.VMEM)

    def fields(*lead):
        return pltpu.VMEM(lead + (planes, rows, lanes), jnp.float32)

    def by_block(count):
        return pltpu.VMEM(count + (planes, 5, block, lanes), jnp.float32)

    sems = pltpu.SemaphoreType.DMA
    held = [
        pltpu.with_memory_space_constraint(values, pltpu.HBM)
        for values in (velsq, epsilon, delta, tilt, azimuth, forward, adjoint, wavelet, receivers, observed)
    ]
    return pl.pallas_call(
        kernel,
        out_shape=jax.ShapeDtypeStruct((5, planes, block, lanes), jnp.float32),
        in_specs=[anywhere] * 8 + [pl.BlockSpec(memory_space=pltpu.SMEM)] + [anywhere] * 2,
        out_specs=vmem,
        scratch_shapes=[pltpu.SMEM(wavelet.shape, jnp.float32)]
        + [pltpu.VMEM(receivers.shape, jnp.int32), pltpu.VMEM(observed.shape, jnp.float32)]
        + [by_block((blocks,))]
        + [padded] * 3
        + [fields(4), fields(9), fields(6), fields(2), fields(2), by_block((blocks,))]
        + [pltpu.VMEM((2, 2, 5, block, lanes), jnp.float32), by_block((2, 2)), by_block(())]
        + [
            sems((16,)),
            sems((14,)),
            sems((2, blocks)),
            sems((7, 2)),
            sems((7, 2)),
            sems((blocks, 2)),
            sems((blocks, 2)),
            sems((4,)),
            sems((4,)),
            sems((8,)),
            sems((8,)),
            sems(()),
            sems(()),
        ],
        compiler_params=pltpu.CompilerParams(
            collective_id=0, has_side_effects=True, vmem_limit_bytes=40 << 20
        ),
        name="gradient",
    )(*held[:8], source, *held[8:])


def solution(mesh):
    field = P("domain", "shot", None)
    state = P("shot", None, "domain", None, None)
    return jax.shard_map(
        shards,
        mesh=mesh,
        in_specs=(field,) * 5 + (state, state, P("shot", None), P("shot"), P("shot", None), P("shot", None, None)),
        out_specs=P(None, "domain", "shot", None),
        check_vma=False,
    )
```

```python
import functools

import jax
import jax.numpy as jnp
from jax import lax
from jax.experimental import pallas as pl
from jax.experimental.pallas import tpu as pltpu
from jax.sharding import PartitionSpec as P

MESH = pl.DeviceIdType.MESH
TILE = 8
PAD = 8


SIN = (1.0, -1 / 6, 1 / 120, -1 / 5040, 1 / 362880, -1 / 39916800, 1 / 6227020800)
COS = (1.0, -1 / 2, 1 / 24, -1 / 720, 1 / 40320, -1 / 3628800, 1 / 479001600, -1 / 87178291200)


def horner(square, series):
    total = jnp.float32(series[-1])
    for term in series[-2::-1]:
        total = total * square + jnp.float32(term)
    return total


def sin_cos(angle):
    square = angle * angle
    return angle * horner(square, SIN), horner(square, COS)


def sin_cos_wide(angle):
    half_sin, half_cos = sin_cos(0.5 * angle)
    return 2.0 * half_sin * half_cos, 1.0 - 2.0 * half_sin * half_sin


def hessian(pad_ref, row, first, last):
    here = pad_ref[:, pl.ds(row, TILE), :]
    above = pad_ref[:, pl.ds(row + 1, TILE), :]
    below = pad_ref[:, pl.ds(row - 1, TILE), :]

    def ahead(values):
        return jnp.where(last, 0.0, pltpu.roll(values, values.shape[-1] - 1, 2))

    def behind(values):
        return jnp.where(first, 0.0, pltpu.roll(values, 1, 2))

    center = here[1:3]
    twice = 2.0 * center
    along_x = here[2:4] - here[0:2]
    along_y = above[1:3] - below[1:3]
    xx = here[2:4] + here[0:2] - twice
    yy = above[1:3] + below[1:3] - twice
    zz = ahead(center) + behind(center) - twice
    xy = (above[2:4] - above[0:2]) - (below[2:4] - below[0:2])
    xz = ahead(along_x) - behind(along_x)
    yz = ahead(along_y) - behind(along_y)
    return center, (xx, yy, zz, xy, xz, yz)


def times_axis(parts, axis, quarter):
    xx, yy, zz, xy, xz, yz = parts
    return (
        xx * axis[0] + xy * quarter[1] + xz * quarter[2],
        xy * quarter[0] + yy * axis[1] + yz * quarter[2],
        xz * quarter[0] + yz * quarter[1] + zz * axis[2],
    )


def dot3(left, right):
    return left[0] * right[0] + left[1] * right[1] + left[2] * right[2]


def kernel(
    velsq,
    epsilon,
    delta,
    tilt,
    azimuth,
    forward,
    adjoint,
    wavelet_in,
    source,
    receivers_in,
    observed_in,
    out,
    wavelet,
    receivers,
    observed,
    coef,
    pad_pq,
    pad_ab,
    pad_next,
    olds,
    table,
    terms,
    step_a,
    hits,
    grad,
    far,
    near,
    mates,
    local_sem,
    gather_send,
    gather_recv,
    halo_send,
    halo_recv,
    next_send,
    next_recv,
    far_send,
    far_recv,
    near_send,
    near_recv,
    mate_send,
    mate_recv,
):
    shot = lax.axis_index("shot")
    domain = lax.axis_index("domain")
    slabs = lax.axis_size("domain")
    rows = pad_pq.shape[2] - 2 * PAD
    block = coef.shape[3]
    blocks = coef.shape[0]
    lanes = pad_pq.shape[3]
    has_low = domain > 0
    has_high = domain < slabs - 1

    def other(dx, dy):
        return lax.rem(shot // 2 + dx, 4) * 2 + lax.rem(lax.rem(shot, 2) + dy, 2)

    def step_of(place):
        dx = jnp.where(
            (place == 2) | (place == 4), 1, jnp.where((place == 3) | (place == 5), 3, jnp.where(place >= 6, 2, 0))
        )
        dy = jnp.where((place == 1) | (place == 4) | (place == 5) | (place == 7), 1, 0)
        return other(dx, dy)

    locals_ = []

    def local(src, dst):
        copy = pltpu.make_async_copy(src, dst, local_sem.at[len(locals_)])
        copy.start()
        locals_.append(copy)

    for place, field in enumerate((velsq, epsilon, delta, tilt, azimuth)):
        local(field, coef.at[shot, :, place])
    inside = pl.ds(PAD, rows)
    for pad, state in ((pad_pq, forward), (pad_ab, adjoint)):
        for place in range(2):
            local(state.at[0, 2 * place + 1], pad.at[place, pl.ds(1, 2), inside])
    for place, (state, member) in enumerate(((forward, 0), (forward, 2), (adjoint, 0), (adjoint, 2))):
        local(state.at[0, member], olds.at[place])

    for src, dst in ((wavelet_in, wavelet), (receivers_in, receivers), (observed_in, observed)):
        local(src, dst)

    barrier = pltpu.get_barrier_semaphore()
    mate, right, left = other(0, 1), other(1, 0), other(3, 0)
    for peer in (mate, right, left):
        pl.semaphore_signal(barrier, inc=1, device_id=(peer, domain), device_id_type=MESH)

    @pl.when(has_low)
    def _():
        pl.semaphore_signal(barrier, inc=1, device_id=(shot, domain - 1), device_id_type=MESH)

    @pl.when(has_high)
    def _():
        pl.semaphore_signal(barrier, inc=1, device_id=(shot, domain + 1), device_id_type=MESH)

    pads = (pad_pq, pad_ab, pad_next)
    for pad in pads:
        zero = jnp.zeros((2, 4, PAD, lanes), jnp.float32)
        pad[:, :, 0:PAD, :] = zero
        pad[:, :, PAD + rows : 2 * PAD + rows, :] = zero

    @pl.when(jnp.logical_not(has_low))
    def _():
        for pad in pads:
            pad[:, 0, PAD : PAD + rows, :] = jnp.zeros((2, rows, lanes), jnp.float32)

    @pl.when(jnp.logical_not(has_high))
    def _():
        for pad in pads:
            pad[:, 3, PAD : PAD + rows, :] = jnp.zeros((2, rows, lanes), jnp.float32)

    pl.semaphore_wait(barrier, 3 + has_low.astype(jnp.int32) + has_high.astype(jnp.int32))

    def halo(pad, span, send, recv, at):
        down = pltpu.make_async_remote_copy(
            src_ref=pad.at[:, 1, span],
            dst_ref=pad.at[:, 3, span],
            send_sem=send.at[at, 0],
            recv_sem=recv.at[at, 0],
            device_id=(shot, domain - 1),
            device_id_type=MESH,
        )
        up = pltpu.make_async_remote_copy(
            src_ref=pad.at[:, 2, span],
            dst_ref=pad.at[:, 0, span],
            send_sem=send.at[at, 1],
            recv_sem=recv.at[at, 1],
            device_id=(shot, domain + 1),
            device_id_type=MESH,
        )
        return down, up

    def begin(pair):
        pl.when(has_low)(pair[0].start)
        pl.when(has_high)(pair[1].start)

    def arrived(pair):
        pl.when(has_high)(pair[0].wait_recv)
        pl.when(has_low)(pair[1].wait_recv)

    def sent(pair):
        pl.when(has_low)(pair[0].wait_send)
        pl.when(has_high)(pair[1].wait_send)

    halo_pq = halo(pad_pq, inside, halo_send, halo_recv, 0)
    window = 2 * block

    def piece(step, offset, size, at):
        row = pl.multiple_of(lax.rem(shot // 2 + step, 4) * window + offset + PAD, TILE)
        return halo(pad_ab, pl.ds(row, size), halo_send, halo_recv, at)

    halo_ab = (piece(2, 0, window, 1), piece(3, 0, TILE, 2), piece(1, window - TILE, TILE, 3))
    halo_ab_late = (piece(1, 0, window - TILE, 4), piece(3, TILE, window - TILE, 5), piece(0, 0, window, 6))

    def push(part, peer, send_sem, recv_sem):
        return pltpu.make_async_remote_copy(
            src_ref=part,
            dst_ref=part,
            send_sem=send_sem,
            recv_sem=recv_sem,
            device_id=(peer, domain),
            device_id_type=MESH,
        )

    def landed(part, recv_sem):
        pltpu.make_async_copy(part, part, recv_sem).wait()

    def own_part(plane, side):
        return push(coef.at[shot, plane], (mate, right, left)[side], gather_send.at[3 * plane + side], gather_recv.at[plane, (1, 3, 2)[side]])

    def mate_part(plane, side):
        return push(coef.at[mate, plane], (right, left)[side], gather_send.at[6 + 2 * plane + side], gather_recv.at[plane, (5, 4)[side]])

    def far_coef(where, side):
        part = coef.at[other((3, 1)[side], where), side]
        return push(part, (right, left)[side], gather_send.at[10 + 2 * where + side], gather_recv.at[side, 6 + where])

    def pass_far(where):
        for side in range(2):
            owner = other((3, 1)[side], where)
            landed(coef.at[owner, side], gather_recv.at[side, (3, 2)[side] + 2 * where])
            far_coef(where, side).start()

    for copy in locals_[0:5]:
        copy.wait()
    for plane, side in ((0, 0), (0, 1), (1, 2), (1, 0), (1, 1), (0, 2)):
        own_part(plane, side).start()
    for copy in locals_[5:9]:
        copy.wait()
    begin(halo_pq)
    for copy in locals_[13:]:
        copy.wait()

    cells = receivers[...] - domain * (2 * rows * lanes)
    at_row = lax.shift_right_arithmetic(cells, 7)
    at_lane = cells & (lanes - 1)
    count = cells.shape[1]
    lane_of = lax.broadcasted_iota(jnp.int32, (lanes, count), 0)
    by_lane = jnp.where(lane_of == at_lane, 1.0, 0.0)
    recorded = by_lane * observed[0, 1:2, :]
    contract = (((1,), (1,)), ((), ()))
    for plane in range(2):
        row_of = lax.broadcasted_iota(jnp.int32, (rows, count), 0) + plane * rows
        by_row = jnp.where(row_of == at_row, 1.0, 0.0)
        hits[0, plane] = lax.dot_general(
            by_row, by_lane, contract, precision=lax.Precision.HIGHEST, preferred_element_type=jnp.float32
        )
        hits[1, plane] = lax.dot_general(
            by_row, recorded, contract, precision=lax.Precision.HIGHEST, preferred_element_type=jnp.float32
        )

    shape = (2, TILE, lanes)
    lane = lax.broadcasted_iota(jnp.int32, shape, 2)
    first = lane == 0
    last = lane == lanes - 1
    cell = lax.broadcasted_iota(jnp.int32, shape, 0) * (rows * lanes) + lax.broadcasted_iota(jnp.int32, shape, 1) * lanes + lane
    source_at = source[0] - domain * (2 * rows * lanes)

    def at_source(row, amount):
        return jnp.where(cell == source_at - row * lanes, amount, 0.0)

    for plane in range(2):
        landed(coef.at[mate, plane], gather_recv.at[plane, 1])
        mate_part(plane, plane).start()
        mate_part(plane, 1 - plane).start()
    pass_far(0)
    for pair in halo_ab:
        begin(pair)
    for copy in locals_[9:13]:
        copy.wait()
    arrived(halo_pq)

    def next_halo(owner):
        span = pl.ds(pl.multiple_of(owner * block + PAD, TILE), block)
        return halo(pad_next, span, next_send, next_recv, owner)

    def forward_tile(owner, tile):
        inner = pl.ds(pl.multiple_of(tile * TILE, TILE), TILE)
        row = pl.multiple_of(owner * block + tile * TILE, TILE)
        span = pl.ds(row, TILE)
        speed, eps, dlt, til, azi = (coef[owner, :, place, inner, :] for place in range(5))
        sin_t, cos_t = sin_cos(til)
        sin_a, cos_a = sin_cos_wide(azi)
        axis = (sin_t * cos_a, sin_t * sin_a, cos_t)
        turn = (cos_t * cos_a, cos_t * sin_a, -sin_t)
        quarter = tuple(0.25 * part for part in axis)
        stretch = 1.0 + 2.0 * eps
        root = jnp.sqrt(1.0 + 2.0 * dlt)
        for place, values in enumerate(axis + turn + (stretch, root, speed)):
            table[place, :, span, :] = values
        here_p, hess_p = hessian(pad_pq.at[0], row + PAD, first, last)
        here_q, hess_q = hessian(pad_pq.at[1], row + PAD, first, last)
        lean_p = times_axis(hess_p, axis, quarter)
        lean_q = times_axis(hess_q, axis, quarter)
        across = hess_p[0] + hess_p[1] + hess_p[2] - dot3(axis, lean_p)
        axial = dot3(axis, lean_q)
        drive_p = stretch * across + root * axial
        drive_q = root * across + axial
        pulse = at_source(row, wavelet[0, 0])
        here = pl.ds(pl.multiple_of(row + PAD, TILE), TILE)
        pad_next[0, 1:3, here, :] = 2.0 * here_p - olds[0, :, span, :] + speed * drive_p + pulse
        pad_next[1, 1:3, here, :] = 2.0 * here_q - olds[1, :, span, :] + speed * drive_q + pulse
        for place, values in enumerate(
            (
                across,
                axial,
                2.0 * dot3(turn, lean_p),
                2.0 * dot3(turn, lean_q),
                2.0 * (axis[0] * lean_p[1] - axis[1] * lean_p[0]),
                2.0 * (axis[0] * lean_q[1] - axis[1] * lean_q[0]),
            )
        ):
            terms[place, :, span, :] = values

    tiles = block // TILE

    def forward_block(turn_at, carry):
        place = jnp.where(turn_at < 2, turn_at + 2, jnp.where(turn_at < 4, turn_at - 2, turn_at))
        owner = step_of(place)

        @pl.when((place == 2) | (place == 3))
        def _():
            landed(coef.at[owner, place - 2], gather_recv.at[place - 2, place])

        @pl.when(place == 4)
        def _():
            pass_far(1)

        @pl.when((place == 4) | (place == 5))
        def _():
            landed(coef.at[owner, place - 4], gather_recv.at[place - 4, place])

        @pl.when(place >= 6)
        def _():
            for plane in range(2):
                landed(coef.at[owner, plane], gather_recv.at[plane, place])

        lax.fori_loop(0, tiles, lambda tile, c: (forward_tile(owner, tile), c)[1], 0, unroll=4)

        @pl.when(place >= 2)
        def _():
            begin(next_halo(owner))

        return carry

    lax.fori_loop(0, blocks, forward_block, 0)

    for place in range(2):
        begin(next_halo(step_of(place)))
    for pair in halo_ab_late:
        begin(pair)
    for pair in halo_ab:
        arrived(pair)

    def load_table(span):
        values = tuple(table[place, :, span, :] for place in range(9))
        return values[0:3], values[3:6], values[6], values[7], values[8]

    def adjoint_tile(owner, tile):
        row = pl.multiple_of(owner * block + tile * TILE, TILE)
        span = pl.ds(row, TILE)
        axis, _, stretch, root, speed = load_table(span)
        quarter = tuple(0.25 * part for part in axis)
        here_a, hess_a = hessian(pad_ab.at[0], row + PAD, first, last)
        here_b, hess_b = hessian(pad_ab.at[1], row + PAD, first, last)
        across = hess_a[0] + hess_a[1] + hess_a[2] - dot3(axis, times_axis(hess_a, axis, quarter))
        axial = dot3(axis, times_axis(hess_b, axis, quarter))
        step_a[0, :, span, :] = 2.0 * here_a - olds[2, :, span, :] + speed * (stretch * across + root * axial)
        step_a[1, :, span, :] = 2.0 * here_b - olds[3, :, span, :] + speed * (root * across + axial)

    def adjoint_block(place, carry):
        owner = step_of(place)
        lax.fori_loop(0, tiles, lambda tile, c: (adjoint_tile(owner, tile), c)[1], 0, unroll=4)
        return carry

    lax.fori_loop(6, blocks, adjoint_block, 0)

    def halo_in(steps):
        for step, y in steps:
            arrived(next_halo(lax.rem(shot // 2 + step, 4) * 2 + y))

    halo_in(((2, 0), (2, 1), (1, 1), (3, 0)))

    def gradient_tile(owner, tile):
        inner = pl.ds(pl.multiple_of(tile * TILE, TILE), TILE)
        row = pl.multiple_of(owner * block + tile * TILE, TILE)
        span = pl.ds(row, TILE)
        axis, turn, stretch, root, speed = load_table(span)
        quarter = tuple(0.25 * part for part in axis)
        here_p, hess_p = hessian(pad_next.at[0], row + PAD, first, last)
        _, hess_q = hessian(pad_next.at[1], row + PAD, first, last)
        lean_p = times_axis(hess_p, axis, quarter)
        lean_q = times_axis(hess_q, axis, quarter)
        across1 = hess_p[0] + hess_p[1] + hess_p[2] - dot3(axis, lean_p)
        axial1 = dot3(axis, lean_q)
        here = pl.ds(pl.multiple_of(row + PAD, TILE), TILE)
        last_p = 2.0 * here_p - pad_pq[0, 1:3, here, :] + speed * (stretch * across1 + root * axial1)
        last_p = last_p + at_source(row, wavelet[0, 1])
        late_a, late_b = pad_ab[0, 1:3, here, :], pad_ab[1, 1:3, here, :]
        early_a = step_a[0, :, span, :] + (hits[0, :, span, :] * last_p - hits[1, :, span, :])
        early_b = step_a[1, :, span, :]
        across0, axial0, tilt_p0, tilt_q0, spin_p0, spin_q0 = (terms[place, :, span, :] for place in range(6))
        tilt_p1 = 2.0 * dot3(turn, lean_p)
        tilt_q1 = 2.0 * dot3(turn, lean_q)
        spin_p1 = 2.0 * (axis[0] * lean_p[1] - axis[1] * lean_p[0])
        spin_q1 = 2.0 * (axis[0] * lean_q[1] - axis[1] * lean_q[0])
        by_stretch = early_a * across0 + late_a * across1
        by_root = early_a * axial0 + early_b * across0 + late_a * axial1 + late_b * across1
        by_one = early_b * axial0 + late_b * axial1

        def turned(p0, q0, p1, q1):
            return speed * (
                root * (early_a * q0 - early_b * p0 + late_a * q1 - late_b * p1)
                - stretch * (early_a * p0 + late_a * p1)
                + (early_b * q0 + late_b * q1)
            )

        for place, values in enumerate(
            (
                stretch * by_stretch + root * by_root + by_one,
                2.0 * speed * by_stretch,
                speed * by_root / root,
                turned(tilt_p0, tilt_q0, tilt_p1, tilt_q1),
                turned(spin_p0, spin_q0, spin_p1, spin_q1),
            )
        ):
            grad[owner, :, place, inner, :] = values

    def far_part(side, where):
        return pltpu.make_async_remote_copy(
            src_ref=grad.at[other(2, where), side],
            dst_ref=far.at[side, where],
            send_sem=far_send.at[2 * side + where],
            recv_sem=far_recv.at[2 * side + where],
            device_id=((right, left)[side], domain),
            device_id_type=MESH,
        )

    def near_part(side, where, plane):
        return pltpu.make_async_remote_copy(
            src_ref=grad.at[other((1, 3)[side], where), plane],
            dst_ref=near.at[side, where, plane],
            send_sem=near_send.at[4 * side + 2 * where + plane],
            recv_sem=near_recv.at[4 * side + 2 * where + plane],
            device_id=((right, left)[side], domain),
            device_id_type=MESH,
        )

    def pass_sums(where):
        for side in range(2):
            owner = other((1, 3)[side], where)
            far_part(side, where).wait_recv()
            grad[owner, side] = grad[owner, side] + far[side, where]
            near_part(side, where, side).start()

    def gradient_block(turn_at, carry):
        place = jnp.where(
            turn_at < 2,
            7 - turn_at,
            jnp.where(turn_at < 4, turn_at + 2, jnp.where(turn_at < 6, turn_at - 2, 7 - turn_at)),
        )
        owner = step_of(place)

        @pl.when(turn_at == 2)
        def _():
            halo_in(((1, 0), (3, 1), (0, 0), (0, 1)))
            for pair in halo_ab_late:
                arrived(pair)

        @pl.when(turn_at >= 2)
        def _():
            adjoint_block(place, 0)

        lax.fori_loop(0, tiles, lambda tile, c: (gradient_tile(owner, tile), c)[1], 0, unroll=4)
        for where in range(2):

            @pl.when(turn_at == 1 - where)
            def _():
                for side in range(2):
                    far_part(side, where).start()

            for side in range(2):

                @pl.when(turn_at == 4 - 2 * where + side)
                def _():
                    near_part(side, where, 1 - side).start()

            @pl.when(turn_at == 5 - 2 * where)
            def _():
                pass_sums(where)

        return carry

    lax.fori_loop(0, blocks, gradient_block, 0)

    def swap(plane):
        return pltpu.make_async_remote_copy(
            src_ref=grad.at[mate, plane],
            dst_ref=mates.at[plane],
            send_sem=mate_send.at[plane],
            recv_sem=mate_recv.at[plane],
            device_id=(mate, domain),
            device_id_type=MESH,
        )

    for plane in range(2):
        for side in range(3):
            own_part(plane, side).wait_send()
        for side in range(2):
            mate_part(plane, side).wait_send()
            far_coef(plane, side).wait_send()
    sent(halo_pq)
    for pair in halo_ab + halo_ab_late:
        sent(pair)

    def drained(owner, carry):
        sent(next_halo(owner))
        return carry

    lax.fori_loop(0, blocks, drained, 0)

    for plane in range(2):
        for side in range(2):
            near_part(side, 1, plane).wait_recv()
        grad[mate, plane] = grad[mate, plane] + (near[0, 1, plane] + near[1, 1, plane])
        swap(plane).start()
    for side in range(2):
        for plane in range(2):
            near_part(side, 0, plane).wait_recv()
    total = grad[shot] + (near[0, 0] + near[1, 0])
    for plane in range(2):
        swap(plane).wait_recv()
        out[:, plane] = total[plane] + mates[plane]

    for side in range(2):
        for where in range(2):
            far_part(side, where).wait_send()
            for plane in range(2):
                near_part(side, where, plane).wait_send()
    for plane in range(2):
        swap(plane).wait_send()


def shards(velsq, epsilon, delta, tilt, azimuth, forward, adjoint, wavelet, source, receivers, observed):
    planes, block, lanes = velsq.shape
    rows = forward.shape[3]
    blocks = rows // block
    padded = pltpu.VMEM((2, planes + 2, rows + 2 * PAD, lanes), jnp.float32)
    anywhere = pl.BlockSpec(memory_space=pl.ANY)
    vmem = pl.BlockSpec(memory_space=pltpu.VMEM)

    def fields(*lead):
        return pltpu.VMEM(lead + (planes, rows, lanes), jnp.float32)

    def by_block(count):
        return pltpu.VMEM(count + (planes, 5, block, lanes), jnp.float32)

    sems = pltpu.SemaphoreType.DMA
    held = [
        pltpu.with_memory_space_constraint(values, pltpu.HBM)
        for values in (velsq, epsilon, delta, tilt, azimuth, forward, adjoint, wavelet, receivers, observed)
    ]
    return pl.pallas_call(
        kernel,
        out_shape=jax.ShapeDtypeStruct((5, planes, block, lanes), jnp.float32),
        in_specs=[anywhere] * 8 + [pl.BlockSpec(memory_space=pltpu.SMEM)] + [anywhere] * 2,
        out_specs=vmem,
        scratch_shapes=[pltpu.SMEM(wavelet.shape, jnp.float32)]
        + [pltpu.VMEM(receivers.shape, jnp.int32), pltpu.VMEM(observed.shape, jnp.float32)]
        + [by_block((blocks,))]
        + [padded] * 3
        + [fields(4), fields(9), fields(6), fields(2), fields(2), by_block((blocks,))]
        + [pltpu.VMEM((2, 2, 5, block, lanes), jnp.float32), by_block((2, 2)), by_block(())]
        + [
            sems((16,)),
            sems((14,)),
            sems((2, blocks)),
            sems((7, 2)),
            sems((7, 2)),
            sems((blocks, 2)),
            sems((blocks, 2)),
            sems((4,)),
            sems((4,)),
            sems((8,)),
            sems((8,)),
            sems((2,)),
            sems((2,)),
        ],
        compiler_params=pltpu.CompilerParams(
            collective_id=0, has_side_effects=True, vmem_limit_bytes=40 << 20
        ),
        name="gradient",
    )(*held[:8], source, *held[8:])


def solution(mesh):
    field = P("domain", "shot", None)
    state = P("shot", None, "domain", None, None)
    return jax.shard_map(
        shards,
        mesh=mesh,
        in_specs=(field,) * 5 + (state, state, P("shot", None), P("shot"), P("shot", None), P("shot", None, None)),
        out_specs=P(None, "domain", "shot", None),
        check_vma=False,
    )
```
